256 devices in a mesh: seg: 8 (over x_hi, y), elem: 32 (over x_lo, z, core).
Axes of the slice: x: 4 (x_hi: 2, x_lo: 2; x = x_hi * 2 + x_lo), y: 4, z: 8, core: 2. Of those that a mesh axis runs over, the one named last changes fastest.
Arguments:
- base_flow: float32 [8, 3, 64, 8192], P('seg', None, None, 'elem'), may hold values from -3 to 3
- probe_field: float32 [8, 3, 64, 8192], P('seg', None, None, 'elem'), may hold values from -6 to 6
- neighbours: int32 [6, 8192], P(None, 'elem'), may hold values from 0 to 8191, as said below
- face_codes: int32 [6, 8192], P(None, 'elem'), may hold values from 0 to 23, as said below
- face_counts: int32 [8192], P('elem'), may hold values from 2 to 6
Outputs:
- first_image: float32 [8, 3, 64, 8192], P('seg', None, None, 'elem')
- second_image: float32 [8, 3, 64, 8192], P('seg', None, None, 'elem')
The draws below stay inside these ranges and needn't reach their ends.
Inputs may be any that keep to these rules, and one draw needn't show every extreme that they name: `neighbours`: every element's neighbour in every slot, used or not, lies within 64 places of the element's own index, counted cyclically over 8192. `face_codes`: each code is 4 times a face number plus a rotation; slots past an element's count hold leftover entries.
All inputs are finite; a program needn't handle non-finite values.
Results may differ from the reference program's by a relative error of at most 0.0001.
Values sent between devices are 32-bit elements; how exact they have to be, the bound alone decides.
A program may use at most 128 MiB of HBM per device.

```python
import jax
import jax.numpy as jnp
import numpy as np
from jax import lax

STEPS = 2
COMP = 3
NODES = 64
HALO = 64
NELEM = 8192
NSEG = 8


def mesh_lists(key):
    base_key = jax.random.fold_in(key, 7)
    key_present, key_offset, key_sign, key_turn = jax.random.split(base_key, 4)
    element_ids = jnp.arange(NELEM, dtype=jnp.int32)
    extra_present = jax.random.randint(key_present, (4, NELEM), 0, 5) < 3
    magnitude = jax.random.randint(key_offset, (4, NELEM), 1, HALO + 1)
    signs = 2 * jax.random.randint(key_sign, (4, NELEM), 0, 2) - 1
    extra_offset = (magnitude * signs).astype(jnp.int32)
    extra_offset = extra_offset.at[0, 0].set(HALO).at[1, 0].set(-HALO)
    extra_present = extra_present.at[:, 0].set(True).at[:, 1].set(False)
    offsets = jnp.concatenate([jnp.full((1, NELEM), -1, jnp.int32), jnp.full((1, NELEM), 1, jnp.int32), extra_offset], axis=0)
    present = jnp.concatenate([jnp.ones((2, NELEM), bool), extra_present], axis=0)
    turns = jax.random.randint(key_turn, (6, NELEM), 0, 4).astype(jnp.int32)
    turns = turns.at[0, 0].set(0).at[5, 0].set(3)
    face_rows = jnp.arange(6, dtype=jnp.int32)[:, None]
    order_key = jnp.where(present, face_rows, face_rows + 8)
    ordering = jnp.argsort(order_key, axis=0, stable=True)
    targets = jnp.mod(element_ids[None, :] + offsets, NELEM).astype(jnp.int32)
    neighbours = jnp.take_along_axis(targets, ordering, axis=0)
    face_codes = jnp.take_along_axis(face_rows * 4 + turns, ordering, axis=0).astype(jnp.int32)
    face_counts = jnp.sum(present.astype(jnp.int32), axis=0).astype(jnp.int32)
    return (neighbours, face_codes, face_counts)


def draw_neighbours(key, part):
    return mesh_lists(key)[0]


def draw_face_codes(key, part):
    return mesh_lists(key)[1]


def draw_face_counts(key, part):
    return mesh_lists(key)[2]


def block_levels(rng, extent, cuts, low, top_value):
    level, own = 1.0, jax.random.fold_in(rng, 6)
    for dim, shards_of in cuts:
        heights = jnp.exp(jax.random.uniform(jax.random.fold_in(own, dim), (shards_of,), jnp.float32, low / len(cuts), top_value / len(cuts)))
        level = level * jnp.repeat(heights, extent[dim] // shards_of).reshape([-1 if axis == dim else 1 for axis in range(len(extent))])
    return level


def scatter_about(key, extent, deviation, most, cuts=(), held_as=jnp.bfloat16):
    entries = jax.random.normal(key, extent, jnp.float32) * deviation
    if len(cuts) > 0:
        entries = block_levels(key, extent, cuts, -0.22, 0.18) * entries
    return jnp.clip(entries, min=-most, max=most).astype(held_as)


def setup_inputs(seed: int = 0) -> dict:
    key_of = jax.random.split(jax.random.key(seed), 6)
    base_flow = scatter_about(key_of[0], (NSEG, COMP, NODES, NELEM), 0.5, 3.0, ((0, 8), (3, 32)), jnp.float32)
    probe_field = scatter_about(key_of[1], (NSEG, COMP, NODES, NELEM), 1.0, 6.0, ((0, 8), (3, 32)), jnp.float32)
    neighbours = draw_neighbours(jax.random.fold_in(key_of[5], 71), 0)
    face_codes = draw_face_codes(jax.random.fold_in(key_of[5], 71), 0)
    face_counts = draw_face_counts(jax.random.fold_in(key_of[5], 71), 0)
    return dict(base_flow=base_flow, probe_field=probe_field, neighbours=neighbours, face_codes=face_codes, face_counts=face_counts)


VISCOSITY = 0.05
PENALTY = 1.0
TIME_STEP = 0.05

def operator_tables():
    points = np.array([-1.0, -1.0 / np.sqrt(5.0), 1.0 / np.sqrt(5.0), 1.0])
    barycentric = np.array([1.0 / np.prod([points[row] - points[col] for col in range(4) if col != row]) for row in range(4)])
    derivative = np.zeros((4, 4))
    for row in range(4):
        for col in range(4):
            if row != col:
                derivative[row, col] = barycentric[col] / barycentric[row] / (points[row] - points[col])
        derivative[row, row] = -np.sum(derivative[row])
    identity = np.eye(4)
    gradient = np.stack([np.kron(np.kron(derivative, identity), identity), np.kron(np.kron(identity, derivative), identity), np.kron(np.kron(identity, identity), derivative)])
    laplacian = gradient[0] @ gradient[0] + gradient[1] @ gradient[1] + gradient[2] @ gradient[2]
    return (jnp.asarray(gradient, jnp.float32), jnp.asarray(laplacian, jnp.float32))

def face_trace(node_grid, which_face):
    direction = which_face // 2
    position = 0 if which_face % 2 == 0 else 3
    return jnp.take(node_grid, position, axis=1 + direction)

def face_lift(values, which_face):
    direction = which_face // 2
    position = 0 if which_face % 2 == 0 else 3
    expanded = jnp.expand_dims(values, 1 + direction)
    widths = [(0, 0)] * 5
    widths[1 + direction] = (position, 3 - position)
    return jnp.pad(expanded, widths)

def face_flux(flow_field, source_field, lookup, face_codes, live_slots):
    node_grid = flow_field.reshape(3, 4, 4, 4, -1)
    own_faces = [face_trace(node_grid, which_face) for which_face in range(6)]
    face_jumps = [jnp.zeros_like(own_faces[0]) for which_face in range(6)]
    for slot_index in range(6):
        neighbour_grid = jnp.take(source_field, lookup[slot_index], axis=2).reshape(3, 4, 4, 4, -1)
        face_number = face_codes[slot_index] // 4
        rotation = face_codes[slot_index] % 4
        opposite = face_trace(neighbour_grid, 1)
        for which_face in range(1, 6):
            opposite = jnp.where(face_number == which_face, face_trace(neighbour_grid, which_face ^ 1), opposite)
        turned = opposite
        for quarter in range(1, 4):
            turned = jnp.where(rotation == quarter, jnp.rot90(opposite, quarter, axes=(1, 2)), turned)
        for which_face in range(6):
            selected = jnp.logical_and(face_number == which_face, live_slots[slot_index])
            face_jumps[which_face] = face_jumps[which_face] + jnp.where(selected, turned - own_faces[which_face], 0.0)
    flux_total = face_lift(face_jumps[0], 0)
    for which_face in range(1, 6):
        flux_total = flux_total + face_lift(face_jumps[which_face], which_face)
    return flux_total.reshape(3, 64, -1)

def operate(flow_field, source_field, base_part, base_grad, lookup, face_codes, live_slots):
    gradient, laplacian_table = operator_tables()
    laplacian = jnp.einsum('mn,cne->cme', laplacian_table, flow_field, precision=lax.Precision.HIGHEST)
    gradients = jnp.einsum('dmn,cne->dcme', gradient, flow_field, precision=lax.Precision.HIGHEST)
    carried = lax.optimization_barrier(jnp.sum(base_part[:, None] * gradients, axis=0))
    stretched = lax.optimization_barrier(jnp.sum(flow_field[:, None] * base_grad, axis=0))
    flux = face_flux(flow_field, source_field, lookup, face_codes, live_slots)
    return VISCOSITY * laplacian - carried - stretched + PENALTY * flux

def segment_flow(flow_field, base_part, neighbours, face_codes, live_slots):
    gradient, laplacian_table = operator_tables()
    base_grad = jnp.einsum('dmn,cne->dcme', gradient, base_part, precision=lax.Precision.HIGHEST)
    for step_index in range(STEPS):
        flow_field = flow_field + TIME_STEP * operate(flow_field, flow_field, base_part, base_grad, neighbours, face_codes, live_slots)
    return flow_field

def reference(base_flow, probe_field, neighbours, face_codes, face_counts):
    live_slots = jnp.arange(6, dtype=jnp.int32)[:, None] < face_counts[None, :]

    def flow_all(input_field):
        return lax.map(lambda segment_pair: segment_flow(segment_pair[0], segment_pair[1], neighbours, face_codes, live_slots), (input_field, base_flow))
    first_image = flow_all(probe_field) - jnp.roll(probe_field, -1, axis=0)
    second_image = flow_all(first_image) - jnp.roll(first_image, -1, axis=0)
    return (first_image, second_image)
```

```python
import functools

import jax
import jax.numpy as jnp
import ml_dtypes
import numpy as np
from jax import lax
from jax.experimental import pallas as pl
from jax.experimental.pallas import tpu as pltpu
from jax.sharding import PartitionSpec as P

STEPS = 2
VISCOSITY = 0.05
PENALTY = 1.0
TIME_STEP = 0.05

COMP = 3
NODES = 64
SHARD = 256
LANES = 128
HALO = 64
CODES = 24


def operator_tables():
    points = np.array([-1.0, -1.0 / np.sqrt(5.0), 1.0 / np.sqrt(5.0), 1.0])
    barycentric = np.array(
        [
            1.0 / np.prod([points[row] - points[col] for col in range(4) if col != row])
            for row in range(4)
        ]
    )
    derivative = np.zeros((4, 4))
    for row in range(4):
        for col in range(4):
            if row != col:
                derivative[row, col] = (
                    barycentric[col] / barycentric[row] / (points[row] - points[col])
                )
        derivative[row, row] = -np.sum(derivative[row])
    identity = np.eye(4)
    gradient = [
        np.kron(np.kron(derivative, identity), identity),
        np.kron(np.kron(identity, derivative), identity),
        np.kron(np.kron(identity, identity), derivative),
    ]
    laplacian = sum(table @ table for table in gradient)
    return gradient, laplacian


def face_nodes(which_face):
    grid = np.arange(NODES).reshape(4, 4, 4)
    return np.take(grid, 0 if which_face % 2 == 0 else 3, axis=which_face // 2)


def constant_tables():
    gradient, laplacian = operator_tables()
    stacked = np.concatenate([VISCOSITY * laplacian] + gradient, axis=0)
    high = stacked.astype(ml_dtypes.bfloat16)
    low = (stacked - high.astype(np.float64)).astype(ml_dtypes.bfloat16)
    operators = np.concatenate([high, high, low, low], axis=1)
    select = np.zeros((CODES * 16, NODES))
    lift = np.zeros((NODES, 96))
    for face in range(6):
        for turn in range(4):
            nodes = np.rot90(face_nodes(face ^ 1), turn).ravel()
            for place, node in enumerate(nodes):
                select[(4 * face + turn) * 16 + place, node] = 1.0
        for place, node in enumerate(face_nodes(face).ravel()):
            lift[node, face * 16 + place] = 1.0
    lift = np.concatenate([lift, lift], axis=1)
    return (
        jnp.asarray(operators),
        jnp.asarray(select.astype(ml_dtypes.bfloat16)),
        jnp.asarray(lift.astype(ml_dtypes.bfloat16)),
    )


def split(value):
    high = value.astype(jnp.bfloat16)
    low = (value - high.astype(jnp.float32)).astype(jnp.bfloat16)
    return high, low


def dot(left, right):
    return jnp.dot(left, right, preferred_element_type=jnp.float32)


def kernel(
    segs,
    elems,
    base_ref,
    probe_ref,
    near_ref,
    code_ref,
    count_ref,
    oper_ref,
    sel_ref,
    lift_ref,
    first_ref,
    second_ref,
    state,
    acc,
    base_grad,
    own_count,
    gather,
    traces,
    jumps,
    mixed,
    send_buf,
    halo_buf,
    follow,
    halo_send,
    halo_recv,
    follow_send,
    follow_recv,
):
    seg = lax.axis_index("seg")
    elem = lax.axis_index("elem")
    right = lax.rem(elem + 1, elems)
    left = lax.rem(elem + elems - 1, elems)
    ahead = lax.rem(seg + 1, segs)
    behind = lax.rem(seg + segs - 1, segs)
    barrier = pltpu.get_barrier_semaphore()
    for target in ({"elem": left}, {"elem": right}, {"seg": ahead}):
        pl.semaphore_signal(
            barrier, inc=1, device_id=target, device_id_type=pl.DeviceIdType.MESH
        )

    lane_low = lax.broadcasted_iota(jnp.int32, (96, LANES), 1) < HALO

    def halo_copy(step, side):
        return pltpu.make_async_remote_copy(
            src_ref=send_buf.at[step, side],
            dst_ref=halo_buf.at[step, side],
            send_sem=halo_send.at[step, side],
            recv_sem=halo_recv.at[step, side],
            device_id={"elem": (right, left)[side]},
            device_id_type=pl.DeviceIdType.MESH,
        )

    def pack_halo(step):
        upper = state[96:192, LANES:SHARD]
        send_buf[step, 0] = jnp.where(
            lane_low, pltpu.roll(upper, HALO, 1), state[0:96, LANES:SHARD]
        )
        lower = state[96:192, 0:LANES]
        send_buf[step, 1] = jnp.where(
            lane_low, state[0:96, 0:LANES], pltpu.roll(lower, HALO, 1)
        )

    def follow_copy(image, source):
        return pltpu.make_async_remote_copy(
            src_ref=source,
            dst_ref=follow.at[image],
            send_sem=follow_send.at[image],
            recv_sem=follow_recv.at[image],
            device_id={"seg": behind},
            device_id_type=pl.DeviceIdType.MESH,
        )

    state[...] = probe_ref[...].reshape(COMP * NODES, SHARD)
    pack_halo(0)
    pl.semaphore_wait(barrier, 3)
    for side in range(2):
        halo_copy(0, side).start()
    follow_copy(0, probe_ref).start()

    first_block = elem * (SHARD // LANES)
    rows16 = lax.broadcasted_iota(jnp.int32, (LANES, LANES), 0)
    for block in range(2):
        lanes = slice(block * LANES, (block + 1) * LANES)
        near = near_ref[:, lanes]
        count = count_ref[:, lanes]
        slot = lax.broadcasted_iota(jnp.int32, (6, LANES), 0)
        code = jnp.where(slot < count, code_ref[:, lanes], -1)
        place = jnp.bitwise_and(near, LANES - 1)
        is_own = jnp.right_shift(near, 7) == first_block + block
        for part in range(2):
            chosen = jnp.where(is_own, place, -1) if part == 0 else jnp.where(is_own, -1, place)
            hot = [
                jnp.where(rows16 == chosen[k : k + 1], 1.0, 0.0).astype(jnp.bfloat16)
                for k in range(6)
            ]

            def build(which, carry):
                total = None
                for k in range(6):
                    match = jnp.where(code[k : k + 1] == which, 1.0, 0.0)
                    match = jnp.broadcast_to(match, (16, LANES)).astype(jnp.bfloat16)
                    match = jnp.concatenate([match] * 8, axis=0)
                    term = hot[k] * match
                    total = term if total is None else total + term
                gather[part, block, which] = total
                return carry

            lax.fori_loop(0, CODES, build, 0)
        node = lax.broadcasted_iota(jnp.int32, (NODES, LANES), 0)
        digits = (
            jnp.right_shift(node, 4),
            jnp.bitwise_and(jnp.right_shift(node, 2), 3),
            jnp.bitwise_and(node, 3),
        )
        total = jnp.zeros((NODES, LANES), jnp.float32)
        for face in range(6):
            hits = jnp.zeros((1, LANES), jnp.float32)
            for k in range(6):
                match = jnp.logical_and(
                    code[k : k + 1] >= 4 * face, code[k : k + 1] < 4 * face + 4
                )
                hits = hits + jnp.where(match, 1.0, 0.0)
            on_face = digits[face // 2] == (0 if face % 2 == 0 else 3)
            total = total + jnp.where(on_face, hits, 0.0)
        own_count[:, lanes] = total

    def derivatives(high, low):
        return dot(oper_ref[...], jnp.concatenate([high, low, high, low], axis=0))

    for comp in range(COMP):
        high, low = split(base_ref[comp])
        grads = derivatives(high, low)
        for d in range(3):
            base_grad[d, comp] = grads[(d + 1) * NODES : (d + 2) * NODES]

    def fill_traces(comp, high, low):
        for piece, value in enumerate((high, low)):
            picked = dot(sel_ref[...], value).astype(jnp.bfloat16)
            traces[:, 2 * comp + piece] = picked.reshape(CODES, 16, SHARD)

    def gather_jumps(part):
        for face in range(6):
            for block in range(2):
                lanes = slice(block * LANES, (block + 1) * LANES)
                sources = jnp.concatenate(
                    [
                        traces[4 * face + turn, :, :, lanes].reshape(96, LANES)
                        for turn in range(4)
                    ],
                    axis=1,
                )
                table = gather[part, block, 4 * face : 4 * face + 4].reshape(4 * LANES, LANES)
                found = dot(sources, table)
                for comp in range(COMP):
                    value = (
                        found[32 * comp : 32 * comp + 16] + found[32 * comp + 16 : 32 * comp + 32]
                    )
                    rows = slice(16 * face, 16 * face + 16)
                    if part == 0:
                        jumps[comp, rows, lanes] = value
                    else:
                        jumps[comp, rows, lanes] += value

    def advance(step, carry):
        for comp in range(COMP):
            field = state[comp * NODES : (comp + 1) * NODES]
            high, low = split(field)
            grads = derivatives(high, low)
            total = grads[0:NODES] - own_count[...] * field
            for d in range(3):
                total = total - base_ref[d] * grads[(d + 1) * NODES : (d + 2) * NODES]
            for d in range(3):
                total = total - state[d * NODES : (d + 1) * NODES] * base_grad[d, comp]
            acc[comp] = total
            fill_traces(comp, high, low)
        gather_jumps(0)

        for side in range(2):
            halo_copy(step, side).wait()
        from_left = halo_buf[step, 0]
        from_right = halo_buf[step, 1]
        mixed[0:96, 0:LANES] = jnp.where(lane_low, state[0:96, LANES:SHARD], from_left)
        mixed[96:192, 0:LANES] = jnp.where(
            lane_low, state[96:192, LANES:SHARD], pltpu.roll(from_left, HALO, 1)
        )
        mixed[0:96, LANES:SHARD] = jnp.where(lane_low, from_right, state[0:96, 0:LANES])
        mixed[96:192, LANES:SHARD] = jnp.where(
            lane_low, pltpu.roll(from_right, HALO, 1), state[96:192, 0:LANES]
        )
        for comp in range(COMP):
            high, low = split(mixed[comp * NODES : (comp + 1) * NODES])
            fill_traces(comp, high, low)
        gather_jumps(1)

        for comp in range(COMP):
            high, low = split(jumps[comp])
            flux = dot(lift_ref[...], jnp.concatenate([high, low], axis=0))
            rows = slice(comp * NODES, (comp + 1) * NODES)
            state[rows] = state[rows] + TIME_STEP * (acc[comp] + PENALTY * flux)

        for image, result in enumerate((first_ref, second_ref)):

            @pl.when(step == STEPS * (image + 1) - 1)
            def _():
                source = probe_ref if image == 0 else first_ref
                follow_copy(image, source).wait()
                value = state[...] - follow[image].reshape(COMP * NODES, SHARD)
                result[...] = value.reshape(COMP, NODES, SHARD)
                if image == 0:
                    state[...] = value
                    follow_copy(1, first_ref).start()

        @pl.when(step < 2 * STEPS - 1)
        def _():
            pack_halo(step + 1)
            for side in range(2):
                halo_copy(step + 1, side).start()

        return carry

    lax.fori_loop(0, 2 * STEPS, advance, 0)


def on_device(base_flow, probe_field, neighbours, face_codes, face_counts):
    operators, select, lift = constant_tables()
    field = jax.ShapeDtypeStruct((COMP, NODES, SHARD), jnp.float32)
    vmem = pl.BlockSpec(memory_space=pltpu.VMEM)
    first_image, second_image = pl.pallas_call(
        functools.partial(kernel, lax.axis_size("seg"), lax.axis_size("elem")),
        out_shape=(field, field),
        in_specs=[vmem] * 8,
        out_specs=(vmem, vmem),
        scratch_shapes=[
            pltpu.VMEM((COMP * NODES, SHARD), jnp.float32),
            pltpu.VMEM((COMP, NODES, SHARD), jnp.float32),
            pltpu.VMEM((3, COMP, NODES, SHARD), jnp.float32),
            pltpu.VMEM((NODES, SHARD), jnp.float32),
            pltpu.VMEM((2, 2, CODES, LANES, LANES), jnp.bfloat16),
            pltpu.VMEM((CODES, 2 * COMP, 16, SHARD), jnp.bfloat16),
            pltpu.VMEM((COMP, 96, SHARD), jnp.float32),
            pltpu.VMEM((COMP * NODES, SHARD), jnp.float32),
            pltpu.VMEM((2 * STEPS, 2, 96, LANES), jnp.float32),
            pltpu.VMEM((2 * STEPS, 2, 96, LANES), jnp.float32),
            pltpu.VMEM((2, COMP, NODES, SHARD), jnp.float32),
            pltpu.SemaphoreType.DMA((2 * STEPS, 2)),
            pltpu.SemaphoreType.DMA((2 * STEPS, 2)),
            pltpu.SemaphoreType.DMA((2,)),
            pltpu.SemaphoreType.DMA((2,)),
        ],
        compiler_params=pltpu.CompilerParams(
            collective_id=0, has_side_effects=True, vmem_limit_bytes=40 * 1024 * 1024
        ),
        name="shooting",
    )(
        base_flow[0],
        probe_field[0],
        neighbours,
        face_codes,
        face_counts.reshape(1, SHARD),
        operators,
        select,
        lift,
    )
    return (first_image[None], second_image[None])


def solution(mesh):
    placed = (
        P("seg", None, None, "elem"),
        P("seg", None, None, "elem"),
        P(None, "elem"),
        P(None, "elem"),
        P("elem"),
    )
    return jax.shard_map(
        on_device,
        mesh=mesh,
        in_specs=placed,
        out_specs=(P("seg", None, None, "elem"), P("seg", None, None, "elem")),
        check_vma=False,
    )
```

```python
import functools

import jax
import jax.numpy as jnp
import ml_dtypes
import numpy as np
from jax import lax
from jax.experimental import pallas as pl
from jax.experimental.pallas import tpu as pltpu
from jax.sharding import PartitionSpec as P

STEPS = 2
VISCOSITY = 0.05
PENALTY = 1.0
TIME_STEP = 0.05

COMP = 3
NODES = 64
SHARD = 256
LANES = 128
HALO = 64
CODES = 24
TRACES = 24


def operator_tables():
    points = np.array([-1.0, -1.0 / np.sqrt(5.0), 1.0 / np.sqrt(5.0), 1.0])
    barycentric = np.array(
        [
            1.0 / np.prod([points[row] - points[col] for col in range(4) if col != row])
            for row in range(4)
        ]
    )
    derivative = np.zeros((4, 4))
    for row in range(4):
        for col in range(4):
            if row != col:
                derivative[row, col] = (
                    barycentric[col] / barycentric[row] / (points[row] - points[col])
                )
        derivative[row, row] = -np.sum(derivative[row])
    identity = np.eye(4)
    gradient = [
        np.kron(np.kron(derivative, identity), identity),
        np.kron(np.kron(identity, derivative), identity),
        np.kron(np.kron(identity, identity), derivative),
    ]
    laplacian = sum(table @ table for table in gradient)
    return gradient, laplacian


def face_nodes(which_face):
    grid = np.arange(NODES).reshape(4, 4, 4)
    return np.take(grid, 0 if which_face % 2 == 0 else 3, axis=which_face // 2)


def orbit_places():
    turned = np.rot90(np.arange(16).reshape(4, 4), 1).ravel()
    seen, starts = set(), []
    for place in range(16):
        if place not in seen:
            starts.append(place)
            for _ in range(4):
                seen.add(place)
                place = turned[place]
    rows = [starts]
    for _ in range(3):
        rows.append([turned[place] for place in rows[-1]])
    return np.array(rows).ravel()


def constant_tables():
    gradient, laplacian = operator_tables()
    stacked = np.concatenate([VISCOSITY * laplacian] + gradient, axis=0)
    high = stacked.astype(ml_dtypes.bfloat16)
    low = (stacked - high.astype(np.float64)).astype(ml_dtypes.bfloat16)
    operators = np.concatenate([high, high, low, low], axis=1)
    places = orbit_places()
    select = np.zeros((2, 6, 2, 2, 8, 2, NODES))
    lift = np.zeros((NODES, 96))
    for face in range(6):
        source = face_nodes(face ^ 1).ravel()[places]
        target = face_nodes(face).ravel()[places]
        for turn in range(2):
            for place in range(16):
                node = source[(place + 4 * turn) % 16]
                for piece in range(2):
                    select[turn, face, place // 8, piece, place % 8, piece, node] = 1.0
        for place in range(16):
            lift[target[place], face * 16 + place] = 1.0
    select = select.reshape(TRACES * 16, 2 * NODES)
    lift = np.concatenate([lift, lift], axis=1)
    return (
        jnp.asarray(operators),
        jnp.asarray(select.astype(ml_dtypes.bfloat16)),
        jnp.asarray(lift.astype(ml_dtypes.bfloat16)),
    )


def split(value):
    high = value.astype(jnp.bfloat16)
    low = (value - high.astype(jnp.float32)).astype(jnp.bfloat16)
    return high, low


def dot(left, right):
    return jnp.dot(left, right, preferred_element_type=jnp.float32)


def kernel(
    segs,
    elems,
    base_in,
    probe_in,
    near_in,
    code_in,
    count_in,
    oper_in,
    sel_in,
    lift_in,
    first_ref,
    second_ref,
    base_ref,
    probe_ref,
    near_ref,
    code_ref,
    count_ref,
    oper_ref,
    sel_ref,
    lift_ref,
    state,
    acc,
    base_grad,
    own_count,
    gather_own,
    gather_halo,
    trace_own,
    trace_halo,
    jumps,
    send_buf,
    halo_buf,
    follow,
    input_sem,
    halo_send,
    halo_recv,
    follow_send,
    follow_recv,
):
    seg = lax.axis_index("seg")
    elem = lax.axis_index("elem")
    right = lax.rem(elem + 1, elems)
    left = lax.rem(elem + elems - 1, elems)
    ahead = lax.rem(seg + 1, segs)
    behind = lax.rem(seg + segs - 1, segs)
    barrier = pltpu.get_barrier_semaphore()
    for target in ({"elem": left}, {"elem": right}, {"seg": ahead}):
        pl.semaphore_signal(
            barrier, inc=1, device_id=target, device_id_type=pl.DeviceIdType.MESH
        )
    loads = [
        pltpu.make_async_copy(source, target, input_sem.at[index])
        for index, (source, target) in enumerate(
            (
                (probe_in, probe_ref),
                (near_in, near_ref),
                (code_in, code_ref),
                (count_in, count_ref),
                (base_in, base_ref),
                (oper_in, oper_ref),
                (sel_in, sel_ref),
                (lift_in, lift_ref),
            )
        )
    ]
    for load in loads:
        load.start()

    lane_low = lax.broadcasted_iota(jnp.int32, (96, LANES), 1) < HALO

    def halo_copy(step, side):
        return pltpu.make_async_remote_copy(
            src_ref=send_buf.at[step, side],
            dst_ref=halo_buf.at[step, side],
            send_sem=halo_send.at[step, side],
            recv_sem=halo_recv.at[step, side],
            device_id={"elem": (right, left)[side]},
            device_id_type=pl.DeviceIdType.MESH,
        )

    def pack_halo(step):
        upper = state[96:192, LANES:SHARD]
        send_buf[step, 0] = jnp.where(
            lane_low, pltpu.roll(upper, HALO, 1), state[0:96, LANES:SHARD]
        )
        lower = state[96:192, 0:LANES]
        send_buf[step, 1] = jnp.where(
            lane_low, state[0:96, 0:LANES], pltpu.roll(lower, HALO, 1)
        )

    def follow_copy(image, source):
        return pltpu.make_async_remote_copy(
            src_ref=source,
            dst_ref=follow.at[image],
            send_sem=follow_send.at[image],
            recv_sem=follow_recv.at[image],
            device_id={"seg": behind},
            device_id_type=pl.DeviceIdType.MESH,
        )

    loads[0].wait()
    state[...] = probe_ref[...].reshape(COMP * NODES, SHARD)
    pack_halo(0)
    pl.semaphore_wait(barrier, 3)
    for side in range(2):
        halo_copy(0, side).start()
    follow_copy(0, probe_ref).start()

    for load in loads[1:4]:
        load.wait()
    first_block = elem * (SHARD // LANES)
    row = lax.broadcasted_iota(jnp.int32, (LANES, LANES), 0)
    codes, hots = [], []
    for block in range(2):
        lanes = slice(block * LANES, (block + 1) * LANES)
        near = near_ref[:, lanes]
        slot = lax.broadcasted_iota(jnp.int32, (6, LANES), 0)
        codes.append(jnp.where(slot < count_ref[:, lanes], code_ref[:, lanes], -1))
        place = jnp.bitwise_and(near, LANES - 1)
        is_own = jnp.right_shift(near, 7) == first_block + block
        for chosen in (jnp.where(is_own, place, -1), jnp.where(is_own, -1, place)):
            hots.append(
                [
                    jnp.where(row == chosen[k : k + 1], 1.0, 0.0).astype(jnp.bfloat16)
                    for k in range(6)
                ]
            )

    def build(face, carry):
        empty = jnp.zeros((HALO, LANES), jnp.bfloat16)
        for turn in range(4):
            which = 4 * face + turn
            for block in range(2):
                lanes = slice(block * LANES, (block + 1) * LANES)
                matches = []
                for k in range(6):
                    match = jnp.where(codes[block][k : k + 1] == which, 1.0, 0.0)
                    match = jnp.broadcast_to(match, (16, LANES)).astype(jnp.bfloat16)
                    matches.append(jnp.concatenate([match] * 8, axis=0))
                totals = []
                for part in range(2):
                    total = None
                    for k in range(6):
                        term = hots[2 * block + part][k] * matches[k]
                        total = term if total is None else total + term
                    totals.append(total)
                own, mixed = totals
                if block == 0:
                    gather_own[which, 0:128, lanes] = own
                    gather_own[which, 128:192, lanes] = mixed[0:64]
                    gather_own[which, 192:256, lanes] = empty
                    gather_halo[which, 0:64, lanes] = empty
                    gather_halo[which, 64:128, lanes] = mixed[64:128]
                else:
                    gather_own[which, 0:64, lanes] = empty
                    gather_own[which, 64:128, lanes] = mixed[64:128]
                    gather_own[which, 128:256, lanes] = own
                    gather_halo[which, 0:64, lanes] = mixed[0:64]
                    gather_halo[which, 64:128, lanes] = empty
        return carry

    lax.fori_loop(0, 6, build, 0)

    node = lax.broadcasted_iota(jnp.int32, (NODES, LANES), 0)
    digits = (
        jnp.right_shift(node, 4),
        jnp.bitwise_and(jnp.right_shift(node, 2), 3),
        jnp.bitwise_and(node, 3),
    )
    for block in range(2):
        code = codes[block]
        total = jnp.zeros((NODES, LANES), jnp.float32)
        for face in range(6):
            hits = jnp.zeros((1, LANES), jnp.float32)
            for k in range(6):
                match = jnp.logical_and(
                    code[k : k + 1] >= 4 * face, code[k : k + 1] < 4 * face + 4
                )
                hits = hits + jnp.where(match, 1.0, 0.0)
            on_face = digits[face // 2] == (0 if face % 2 == 0 else 3)
            total = total + jnp.where(on_face, hits, 0.0)
        own_count[:, block * LANES : (block + 1) * LANES] = total

    for load in loads[4:8]:
        load.wait()

    def derivatives(high, low):
        return dot(oper_ref[...], jnp.concatenate([high, low, high, low], axis=0))

    for comp in range(COMP):
        high, low = split(base_ref[comp])
        grads = derivatives(high, low)
        for d in range(3):
            base_grad[d, comp] = grads[(d + 1) * NODES : (d + 2) * NODES]

    def fill_traces(traces, comp, high, low):
        picked = dot(sel_ref[...], jnp.concatenate([high, low], axis=0))
        picked = picked.astype(jnp.bfloat16).reshape(TRACES, 16, high.shape[1])
        traces[:, 16 * comp : 16 * comp + 16] = picked

    def gather_jumps(traces, tables, add):
        for face in range(6):
            sources = []
            for turn in range(4):
                pair = 2 * (6 * (turn % 2) + face)
                for half in range(2):
                    sources.append(traces[pair + (half + turn // 2) % 2])
            sources = jnp.concatenate(
                [
                    jnp.concatenate(sources[2 * turn : 2 * turn + 2], axis=0)
                    for turn in range(4)
                ],
                axis=1,
            )
            table = tables[4 * face : 4 * face + 4]
            found = dot(sources, table.reshape(4 * table.shape[1], SHARD))
            for half in range(2):
                for comp in range(COMP):
                    at = 48 * half + 16 * comp
                    value = found[at : at + 8] + found[at + 8 : at + 16]
                    rows = slice(16 * face + 8 * half, 16 * face + 8 * half + 8)
                    if add:
                        value = value + jumps[comp, rows]
                    jumps[comp, rows] = value

    def advance(step, carry):
        for comp in range(COMP):
            field = state[comp * NODES : (comp + 1) * NODES]
            high, low = split(field)
            grads = derivatives(high, low)
            total = grads[0:NODES] - own_count[...] * field
            for d in range(3):
                total = total - base_ref[d] * grads[(d + 1) * NODES : (d + 2) * NODES]
            for d in range(3):
                total = total - state[d * NODES : (d + 1) * NODES] * base_grad[d, comp]
            acc[comp] = total
            fill_traces(trace_own, comp, high, low)
        gather_jumps(trace_own, gather_own, False)

        for side in range(2):
            halo_copy(step, side).wait()
        from_left = halo_buf[step, 0]
        from_right = halo_buf[step, 1]
        halo = jnp.concatenate(
            [
                jnp.where(lane_low, from_right, from_left),
                pltpu.roll(jnp.where(lane_low, from_left, from_right), HALO, 1),
            ],
            axis=0,
        )
        for comp in range(COMP):
            high, low = split(halo[comp * NODES : (comp + 1) * NODES])
            fill_traces(trace_halo, comp, high, low)
        gather_jumps(trace_halo, gather_halo, True)

        for comp in range(COMP):
            high, low = split(jumps[comp])
            flux = dot(lift_ref[...], jnp.concatenate([high, low], axis=0))
            rows = slice(comp * NODES, (comp + 1) * NODES)
            state[rows] = state[rows] + TIME_STEP * (acc[comp] + PENALTY * flux)

        for image, result in enumerate((first_ref, second_ref)):

            @pl.when(step == STEPS * (image + 1) - 1)
            def _():
                source = probe_ref if image == 0 else first_ref
                follow_copy(image, source).wait()
                value = state[...] - follow[image].reshape(COMP * NODES, SHARD)
                result[...] = value.reshape(COMP, NODES, SHARD)
                if image == 0:
                    state[...] = value

        @pl.when(step < 2 * STEPS - 1)
        def _():
            pack_halo(step + 1)
            for side in range(2):
                halo_copy(step + 1, side).start()

        @pl.when(step == STEPS - 1)
        def _():
            follow_copy(1, first_ref).start()

        return carry

    lax.fori_loop(0, 2 * STEPS, advance, 0)


def on_device(base_flow, probe_field, neighbours, face_codes, face_counts):
    operators, select, lift = constant_tables()
    field = jax.ShapeDtypeStruct((COMP, NODES, SHARD), jnp.float32)
    vmem = pl.BlockSpec(memory_space=pltpu.VMEM)
    first_image, second_image = pl.pallas_call(
        functools.partial(kernel, lax.axis_size("seg"), lax.axis_size("elem")),
        out_shape=(field, field),
        in_specs=[pl.BlockSpec(memory_space=pltpu.HBM)] * 8,
        out_specs=(vmem, vmem),
        scratch_shapes=[
            pltpu.VMEM((COMP, NODES, SHARD), jnp.float32),
            pltpu.VMEM((COMP, NODES, SHARD), jnp.float32),
            pltpu.VMEM((6, SHARD), jnp.int32),
            pltpu.VMEM((6, SHARD), jnp.int32),
            pltpu.VMEM((1, SHARD), jnp.int32),
            pltpu.VMEM(operators.shape, jnp.bfloat16),
            pltpu.VMEM(select.shape, jnp.bfloat16),
            pltpu.VMEM(lift.shape, jnp.bfloat16),
            pltpu.VMEM((COMP * NODES, SHARD), jnp.float32),
            pltpu.VMEM((COMP, NODES, SHARD), jnp.float32),
            pltpu.VMEM((3, COMP, NODES, SHARD), jnp.float32),
            pltpu.VMEM((NODES, SHARD), jnp.float32),
            pltpu.VMEM((CODES, SHARD, SHARD), jnp.bfloat16),
            pltpu.VMEM((CODES, LANES, SHARD), jnp.bfloat16),
            pltpu.VMEM((TRACES, 16 * COMP, SHARD), jnp.bfloat16),
            pltpu.VMEM((TRACES, 16 * COMP, LANES), jnp.bfloat16),
            pltpu.VMEM((COMP, 96, SHARD), jnp.float32),
            pltpu.VMEM((2 * STEPS, 2, 96, LANES), jnp.float32),
            pltpu.VMEM((2 * STEPS, 2, 96, LANES), jnp.float32),
            pltpu.VMEM((2, COMP, NODES, SHARD), jnp.float32),
            pltpu.SemaphoreType.DMA((8,)),
            pltpu.SemaphoreType.DMA((2 * STEPS, 2)),
            pltpu.SemaphoreType.DMA((2 * STEPS, 2)),
            pltpu.SemaphoreType.DMA((2,)),
            pltpu.SemaphoreType.DMA((2,)),
        ],
        compiler_params=pltpu.CompilerParams(
            collective_id=0, has_side_effects=True, vmem_limit_bytes=40 * 1024 * 1024
        ),
        name="shooting",
    )(
        *[
            pltpu.with_memory_space_constraint(value, pltpu.HBM)
            for value in (
                base_flow[0],
                probe_field[0],
                neighbours,
                face_codes,
                face_counts.reshape(1, SHARD),
                operators,
                select,
                lift,
            )
        ]
    )
    return (first_image[None], second_image[None])


def solution(mesh):
    placed = (
        P("seg", None, None, "elem"),
        P("seg", None, None, "elem"),
        P(None, "elem"),
        P(None, "elem"),
        P("elem"),
    )
    return jax.shard_map(
        on_device,
        mesh=mesh,
        in_specs=placed,
        out_specs=(P("seg", None, None, "elem"), P("seg", None, None, "elem")),
        check_vma=False,
    )
```

```python
import functools

import jax
import jax.numpy as jnp
import ml_dtypes
import numpy as np
from jax import lax
from jax.experimental import pallas as pl
from jax.experimental.pallas import tpu as pltpu
from jax.sharding import PartitionSpec as P

STEPS = 2
VISCOSITY = 0.05
PENALTY = 1.0
TIME_STEP = 0.05

COMP = 3
NODES = 64
SHARD = 256
LANES = 128
HALO = 64
TRACES = 24


def operator_tables():
    points = np.array([-1.0, -1.0 / np.sqrt(5.0), 1.0 / np.sqrt(5.0), 1.0])
    barycentric = np.array(
        [
            1.0 / np.prod([points[row] - points[col] for col in range(4) if col != row])
            for row in range(4)
        ]
    )
    derivative = np.zeros((4, 4))
    for row in range(4):
        for col in range(4):
            if row != col:
                derivative[row, col] = (
                    barycentric[col] / barycentric[row] / (points[row] - points[col])
                )
        derivative[row, row] = -np.sum(derivative[row])
    identity = np.eye(4)
    gradient = [
        np.kron(np.kron(derivative, identity), identity),
        np.kron(np.kron(identity, derivative), identity),
        np.kron(np.kron(identity, identity), derivative),
    ]
    laplacian = sum(table @ table for table in gradient)
    return gradient, laplacian


def face_nodes(which_face):
    grid = np.arange(NODES).reshape(4, 4, 4)
    return np.take(grid, 0 if which_face % 2 == 0 else 3, axis=which_face // 2)


def orbit_places():
    turned = np.rot90(np.arange(16).reshape(4, 4), 1).ravel()
    seen, starts = set(), []
    for place in range(16):
        if place not in seen:
            starts.append(place)
            for _ in range(4):
                seen.add(place)
                place = turned[place]
    rows = [starts]
    for _ in range(3):
        rows.append([turned[place] for place in rows[-1]])
    return np.array(rows).ravel()


def constant_tables():
    gradient, laplacian = operator_tables()
    stacked = np.concatenate([VISCOSITY * laplacian] + gradient, axis=0)
    high = stacked.astype(ml_dtypes.bfloat16)
    low = (stacked - high.astype(np.float64)).astype(ml_dtypes.bfloat16)
    operators = np.concatenate([high, high, low, low], axis=1)
    places = orbit_places()
    select = np.zeros((2, 6, 2, 2, 8, 2, NODES))
    lift = np.zeros((NODES, 96))
    for face in range(6):
        source = face_nodes(face ^ 1).ravel()[places]
        target = face_nodes(face).ravel()[places]
        for turn in range(2):
            for place in range(16):
                node = source[(place + 4 * turn) % 16]
                for piece in range(2):
                    select[turn, face, place // 8, piece, place % 8, piece, node] = 1.0
        for place in range(16):
            lift[target[place], face * 16 + place] = 1.0
    select = select.reshape(TRACES * 16, 2 * NODES)
    paired = np.concatenate([select[: TRACES * 8], select[TRACES * 8 :]], axis=1)
    lift = np.concatenate([lift, lift], axis=1)
    return (
        jnp.asarray(operators),
        jnp.asarray(select.astype(ml_dtypes.bfloat16)),
        jnp.asarray(paired.astype(ml_dtypes.bfloat16)),
        jnp.asarray(lift.astype(ml_dtypes.bfloat16)),
    )


def split(value):
    high = value.astype(jnp.bfloat16)
    low = (value - high.astype(jnp.float32)).astype(jnp.bfloat16)
    return high, low


def dot(left, right):
    return jnp.dot(left, right, preferred_element_type=jnp.float32)


def kernel(
    segs,
    elems,
    base_in,
    probe_in,
    near_in,
    code_in,
    count_in,
    oper_in,
    sel_in,
    pair_in,
    lift_in,
    first_ref,
    second_ref,
    base_ref,
    probe_ref,
    near_ref,
    code_ref,
    count_ref,
    oper_ref,
    sel_ref,
    pair_ref,
    lift_ref,
    state,
    acc,
    base_grad,
    own_count,
    hot,
    inner,
    outer,
    trace_own,
    trace_cross,
    jumps,
    send_buf,
    halo_buf,
    follow,
    input_sem,
    halo_send,
    halo_recv,
    follow_send,
    follow_recv,
):
    seg = lax.axis_index("seg")
    elem = lax.axis_index("elem")
    right = lax.rem(elem + 1, elems)
    left = lax.rem(elem + elems - 1, elems)
    ahead = lax.rem(seg + 1, segs)
    behind = lax.rem(seg + segs - 1, segs)
    barrier = pltpu.get_barrier_semaphore()
    for target in ({"elem": left}, {"elem": right}, {"seg": ahead}):
        pl.semaphore_signal(
            barrier, inc=1, device_id=target, device_id_type=pl.DeviceIdType.MESH
        )
    loads = [
        pltpu.make_async_copy(source, target, input_sem.at[index])
        for index, (source, target) in enumerate(
            (
                (near_in, near_ref),
                (code_in, code_ref),
                (count_in, count_ref),
                (probe_in, probe_ref),
                (base_in, base_ref),
                (oper_in, oper_ref),
                (sel_in, sel_ref),
                (pair_in, pair_ref),
                (lift_in, lift_ref),
            )
        )
    ]
    for load in loads:
        load.start()

    block_lanes = (slice(0, LANES), slice(LANES, SHARD))
    lane_low = lax.broadcasted_iota(jnp.int32, (96, LANES), 1) < HALO
    low_ones = lax.broadcasted_iota(jnp.int32, (16, LANES), 1) < HALO
    low_ones = jnp.where(low_ones, 1.0, 0.0).astype(jnp.bfloat16)
    keep_high = jnp.concatenate([1.0 - low_ones] * 8, axis=0)
    keep_low = jnp.concatenate([low_ones] * 8, axis=0)

    def halo_copy(step, block):
        return pltpu.make_async_remote_copy(
            src_ref=send_buf.at[step, block],
            dst_ref=halo_buf.at[step, 1 - block],
            send_sem=halo_send.at[step, block],
            recv_sem=halo_recv.at[step, 1 - block],
            device_id={"elem": (left, right)[block]},
            device_id_type=pl.DeviceIdType.MESH,
        )

    def pack_halo(step, block):
        lanes = block_lanes[block]
        upper, lower = state[0:96, lanes], pltpu.roll(state[96:192, lanes], HALO, 1)
        send_buf[step, block] = (
            jnp.where(lane_low, upper, lower)
            if block == 0
            else jnp.where(lane_low, lower, upper)
        )

    def follow_copy(image, source):
        return pltpu.make_async_remote_copy(
            src_ref=source,
            dst_ref=follow.at[image],
            send_sem=follow_send.at[image],
            recv_sem=follow_recv.at[image],
            device_id={"seg": behind},
            device_id_type=pl.DeviceIdType.MESH,
        )

    for load in loads[0:3]:
        load.wait()
    first_block = elem * (SHARD // LANES)
    row = lax.broadcasted_iota(jnp.int32, (LANES, LANES), 0)
    codes = []
    for block in range(2):
        lanes = block_lanes[block]
        slot = lax.broadcasted_iota(jnp.int32, (6, LANES), 0)
        codes.append(jnp.where(slot < count_ref[:, lanes], code_ref[:, lanes], -1))
        place = jnp.bitwise_and(near_ref[:, lanes], LANES - 1)
        is_own = jnp.right_shift(near_ref[:, lanes], 7) == first_block + block
        for part, chosen in enumerate(
            (jnp.where(is_own, place, -1), jnp.where(is_own, -1, place))
        ):
            for k in range(6):
                hot[block, part, k] = jnp.where(row == chosen[k : k + 1], 1.0, 0.0).astype(
                    jnp.bfloat16
                )

    loads[3].wait()
    state[...] = probe_ref[...].reshape(COMP * NODES, SHARD)
    for block in range(2):
        pack_halo(0, block)
    pl.semaphore_wait(barrier, 3)
    for block in range(2):
        halo_copy(0, block).start()
    follow_copy(0, probe_ref).start()

    wide_codes = [
        [jnp.broadcast_to(codes[block][k : k + 1], (8, LANES)) for k in range(6)]
        for block in range(2)
    ]

    def build(face, carry):
        for block in range(2):
            matches = []
            for turn in range(4):
                matches.append([])
                for k in range(6):
                    match = jnp.where(wide_codes[block][k] == 4 * face + turn, 1.0, 0.0)
                    match = jnp.concatenate([match, match], axis=0).astype(jnp.bfloat16)
                    matches[turn].append(match)
            for part in range(2):
                for chunk in range(8):
                    rows = [hot[block, part, k, 16 * chunk : 16 * chunk + 16] for k in range(6)]
                    for turn in range(4):
                        total = rows[0] * matches[turn][0]
                        for k in range(1, 6):
                            total = total + rows[k] * matches[turn][k]
                        if part == 0:
                            at = LANES * turn + 16 * chunk
                            inner[block, face, at : at + 16] = total
                        elif (chunk < 4) == (block == 0):
                            at = 4 * LANES + HALO * turn + 16 * (chunk % 4)
                            inner[block, face, at : at + 16] = total
                        else:
                            at = HALO * turn + 16 * (chunk % 4)
                            outer[block, face, at : at + 16] = total
        return carry

    lax.fori_loop(0, 6, build, 0)

    node = lax.broadcasted_iota(jnp.int32, (NODES, LANES), 0)
    digits = (
        jnp.right_shift(node, 4),
        jnp.bitwise_and(jnp.right_shift(node, 2), 3),
        jnp.bitwise_and(node, 3),
    )
    for block in range(2):
        code = codes[block]
        total = jnp.zeros((NODES, LANES), jnp.float32)
        for face in range(6):
            hits = jnp.zeros((1, LANES), jnp.float32)
            for k in range(6):
                match = jnp.logical_and(
                    code[k : k + 1] >= 4 * face, code[k : k + 1] < 4 * face + 4
                )
                hits = hits + jnp.where(match, 1.0, 0.0)
            on_face = digits[face // 2] == (0 if face % 2 == 0 else 3)
            total = total + jnp.where(on_face, hits, 0.0)
        own_count[:, block_lanes[block]] = total

    for load in loads[4:]:
        load.wait()

    def stacked(value):
        return jnp.concatenate(split(value), axis=0)

    def derivatives(pieces):
        return dot(oper_ref[...], jnp.concatenate([pieces, pieces], axis=0))

    for comp in range(COMP):
        grads = derivatives(stacked(base_ref[comp]))
        for d in range(3):
            base_grad[d, comp] = grads[(d + 1) * NODES : (d + 2) * NODES]

    def fill_pairs(comp, at_low, at_high):
        paired = jnp.concatenate([at_low * keep_low, at_high * keep_high], axis=0)
        picked = dot(pair_ref[...], paired).astype(jnp.bfloat16)
        return picked.reshape(TRACES // 2, 16, LANES)

    def stacked_halves(halves, face, turns):
        pair = 2 * face + 12 * (turns % 2)
        first = pair + turns // 2
        return jnp.concatenate([halves(first), halves(2 * pair + 1 - first)], axis=0)

    def add_pieces(found, comp, half):
        at = 48 * half + 16 * comp
        return found[at : at + 8] + found[at + 8 : at + 16]

    def before_halo():
        for comp in range(COMP):
            field = state[comp * NODES : (comp + 1) * NODES]
            pieces = stacked(field)
            grads = derivatives(pieces)
            total = grads[0:NODES] - own_count[...] * field
            for d in range(3):
                total = total - base_ref[d] * grads[(d + 1) * NODES : (d + 2) * NODES]
            for d in range(3):
                total = total - state[d * NODES : (d + 1) * NODES] * base_grad[d, comp]
            acc[comp] = total
            rows = slice(16 * comp, 16 * comp + 16)
            picked = dot(sel_ref[...], pieces).astype(jnp.bfloat16)
            trace_own[:, rows] = picked.reshape(TRACES, 16, SHARD)
            turned = [stacked(pltpu.roll(field[:, lanes], HALO, 1)) for lanes in block_lanes]
            trace_cross[0, :, rows] = fill_pairs(comp, pieces[:, LANES:SHARD], turned[1])
            trace_cross[1, :, rows] = fill_pairs(comp, turned[0], pieces[:, 0:LANES])
        for block in range(2):
            lanes = block_lanes[block]
            for face in range(6):
                sources = [
                    stacked_halves(lambda at: trace_own[at, :, lanes], face, turn)
                    for turn in range(4)
                ]
                for turn in (0, 2):
                    sources.append(
                        stacked_halves(lambda at: trace_cross[block, at], face, turn)
                    )
                found = dot(jnp.concatenate(sources, axis=1), inner[block, face])
                for half in range(2):
                    at = 16 * face + 8 * half
                    for comp in range(COMP):
                        jumps[comp, at : at + 8, lanes] = add_pieces(found, comp, half)

    def after_halo(step, block):
        lanes = block_lanes[block]
        halo_copy(step, 1 - block).wait_recv()
        packet = halo_buf[step, block]
        turned = pltpu.roll(packet, HALO, 1)
        as_sent = jnp.concatenate([packet, turned], axis=0)
        shifted = jnp.concatenate([turned, packet], axis=0)
        at_high, at_low = (as_sent, shifted) if block == 0 else (shifted, as_sent)
        traces = []
        for comp in range(COMP):
            rows = slice(comp * NODES, (comp + 1) * NODES)
            traces.append(fill_pairs(comp, stacked(at_low[rows]), stacked(at_high[rows])))
        totals = [[] for comp in range(COMP)]
        for face in range(6):
            sources = [
                stacked_halves(
                    lambda at: jnp.concatenate([trace[at] for trace in traces], axis=0),
                    face,
                    turn,
                )
                for turn in (0, 2)
            ]
            found = dot(jnp.concatenate(sources, axis=1), outer[block, face])
            for half in range(2):
                at = 16 * face + 8 * half
                for comp in range(COMP):
                    totals[comp].append(
                        add_pieces(found, comp, half) + jumps[comp, at : at + 8, lanes]
                    )
        last = step % STEPS == STEPS - 1
        image = step // STEPS
        result = (first_ref, second_ref)[image]
        for comp in range(COMP):
            flux = dot(lift_ref[...], stacked(jnp.concatenate(totals[comp], axis=0)))
            rows = slice(comp * NODES, (comp + 1) * NODES)
            value = state[rows, lanes]
            value = value + TIME_STEP * (acc[comp, :, lanes] + PENALTY * flux)
            if last:
                value = value - follow[image, comp, :, lanes]
                result[comp, :, lanes] = value
            if step < 2 * STEPS - 1:
                state[rows, lanes] = value
        if step < 2 * STEPS - 1:
            pack_halo(step + 1, block)
            halo_copy(step + 1, block).start()

    for step in range(2 * STEPS):
        before_halo()
        if step % STEPS == STEPS - 1:
            follow_copy(step // STEPS, first_ref).wait_recv()
        for block in (step % 2, 1 - step % 2):
            after_halo(step, block)
        if step == STEPS - 1:
            follow_copy(1, first_ref).start()
    for step in range(2 * STEPS):
        for block in range(2):
            halo_copy(step, block).wait_send()
    for image, source in enumerate((probe_ref, first_ref)):
        follow_copy(image, source).wait_send()


def on_device(base_flow, probe_field, neighbours, face_codes, face_counts):
    operators, select, paired, lift = constant_tables()
    field = jax.ShapeDtypeStruct((COMP, NODES, SHARD), jnp.float32)
    vmem = pl.BlockSpec(memory_space=pltpu.VMEM)
    first_image, second_image = pl.pallas_call(
        functools.partial(kernel, lax.axis_size("seg"), lax.axis_size("elem")),
        out_shape=(field, field),
        in_specs=[pl.BlockSpec(memory_space=pltpu.HBM)] * 9,
        out_specs=(vmem, vmem),
        scratch_shapes=[
            pltpu.VMEM((COMP, NODES, SHARD), jnp.float32),
            pltpu.VMEM((COMP, NODES, SHARD), jnp.float32),
            pltpu.VMEM((6, SHARD), jnp.int32),
            pltpu.VMEM((6, SHARD), jnp.int32),
            pltpu.VMEM((1, SHARD), jnp.int32),
            pltpu.VMEM(operators.shape, jnp.bfloat16),
            pltpu.VMEM(select.shape, jnp.bfloat16),
            pltpu.VMEM(paired.shape, jnp.bfloat16),
            pltpu.VMEM(lift.shape, jnp.bfloat16),
            pltpu.VMEM((COMP * NODES, SHARD), jnp.float32),
            pltpu.VMEM((COMP, NODES, SHARD), jnp.float32),
            pltpu.VMEM((3, COMP, NODES, SHARD), jnp.float32),
            pltpu.VMEM((NODES, SHARD), jnp.float32),
            pltpu.VMEM((2, 2, 6, LANES, LANES), jnp.bfloat16),
            pltpu.VMEM((2, 6, 4 * (LANES + HALO), LANES), jnp.bfloat16),
            pltpu.VMEM((2, 6, 4 * HALO, LANES), jnp.bfloat16),
            pltpu.VMEM((TRACES, 16 * COMP, SHARD), jnp.bfloat16),
            pltpu.VMEM((2, TRACES // 2, 16 * COMP, LANES), jnp.bfloat16),
            pltpu.VMEM((COMP, 96, SHARD), jnp.float32),
            pltpu.VMEM((2 * STEPS, 2, 96, LANES), jnp.float32),
            pltpu.VMEM((2 * STEPS, 2, 96, LANES), jnp.float32),
            pltpu.VMEM((2, COMP, NODES, SHARD), jnp.float32),
            pltpu.SemaphoreType.DMA((9,)),
            pltpu.SemaphoreType.DMA((2 * STEPS, 2)),
            pltpu.SemaphoreType.DMA((2 * STEPS, 2)),
            pltpu.SemaphoreType.DMA((2,)),
            pltpu.SemaphoreType.DMA((2,)),
        ],
        compiler_params=pltpu.CompilerParams(
            collective_id=0, has_side_effects=True, vmem_limit_bytes=40 * 1024 * 1024
        ),
        name="shooting",
    )(
        *[
            pltpu.with_memory_space_constraint(value, pltpu.HBM)
            for value in (
                base_flow[0],
                probe_field[0],
                neighbours,
                face_codes,
                face_counts.reshape(1, SHARD),
                operators,
                select,
                paired,
                lift,
            )
        ]
    )
    return (first_image[None], second_image[None])


def solution(mesh):
    placed = (
        P("seg", None, None, "elem"),
        P("seg", None, None, "elem"),
        P(None, "elem"),
        P(None, "elem"),
        P("elem"),
    )
    return jax.shard_map(
        on_device,
        mesh=mesh,
        in_specs=placed,
        out_specs=(P("seg", None, None, "elem"), P("seg", None, None, "elem")),
        check_vma=False,
    )
```

```python
import functools

import jax
import jax.numpy as jnp
import ml_dtypes
import numpy as np
from jax import lax
from jax.experimental import pallas as pl
from jax.experimental.pallas import tpu as pltpu
from jax.sharding import PartitionSpec as P

STEPS = 2
VISCOSITY = 0.05
PENALTY = 1.0
TIME_STEP = 0.05

COMP = 3
NODES = 64
SHARD = 256
LANES = 128
HALO = 64
EDGE = 2
SLOTS = 6


def operator_tables():
    points = np.array([-1.0, -1.0 / np.sqrt(5.0), 1.0 / np.sqrt(5.0), 1.0])
    barycentric = np.array(
        [
            1.0 / np.prod([points[row] - points[col] for col in range(4) if col != row])
            for row in range(4)
        ]
    )
    derivative = np.zeros((4, 4))
    for row in range(4):
        for col in range(4):
            if row != col:
                derivative[row, col] = (
                    barycentric[col] / barycentric[row] / (points[row] - points[col])
                )
        derivative[row, row] = -np.sum(derivative[row])
    identity = np.eye(4)
    gradient = [
        np.kron(np.kron(derivative, identity), identity),
        np.kron(np.kron(identity, derivative), identity),
        np.kron(np.kron(identity, identity), derivative),
    ]
    laplacian = sum(table @ table for table in gradient)
    return gradient, laplacian


def operator_pieces():
    gradient, laplacian = operator_tables()
    stacked = np.concatenate([VISCOSITY * laplacian] + gradient, axis=0)
    high = stacked.astype(ml_dtypes.bfloat16)
    low = (stacked - high.astype(np.float64)).astype(ml_dtypes.bfloat16)
    return jnp.asarray(np.concatenate([high, high, low, low], axis=1))


def split(value):
    high = value.astype(jnp.bfloat16)
    low = (value - high.astype(jnp.float32)).astype(jnp.bfloat16)
    return high, low


def dot(left, right):
    return jnp.dot(left, right, preferred_element_type=jnp.float32)


def kernel(
    segs,
    elems,
    base_in,
    probe_in,
    near_in,
    code_in,
    count_in,
    oper_in,
    first_ref,
    second_ref,
    oper_ref,
    near_ref,
    code_ref,
    count_ref,
    near_far,
    code_far,
    count_far,
    base,
    base_pack,
    base_far,
    state,
    acc,
    base_grad,
    own_count,
    places,
    targets,
    table,
    edge_table,
    sources,
    edge_sources,
    halo,
    follow,
    input_sem,
    list_send,
    list_recv,
    base_send,
    base_recv,
    halo_send,
    halo_recv,
    follow_send,
    follow_recv,
):
    seg = lax.axis_index("seg")
    elem = lax.axis_index("elem")
    right = lax.rem(elem + 1, elems)
    left = lax.rem(elem + elems - 1, elems)
    ahead = lax.rem(seg + 1, segs)
    behind = lax.rem(seg + segs - 1, segs)
    barrier = pltpu.get_barrier_semaphore()
    for target in ({"elem": left}, {"elem": right}, {"seg": ahead}):
        pl.semaphore_signal(
            barrier, inc=1, device_id=target, device_id_type=pl.DeviceIdType.MESH
        )
    block_lanes = (slice(0, LANES), slice(LANES, SHARD))
    pairs = [(near_in, near_ref), (code_in, code_ref), (count_in, count_ref)]
    for block in range(2):
        pairs.append((probe_in.at[:, :, block_lanes[block]], state.at[block]))
    for block in range(2):
        pairs.append((base_in.at[:, :, block_lanes[block]], base.at[block]))
    pairs.append((oper_in, oper_ref))
    loads = [
        pltpu.make_async_copy(source, target, input_sem.at[index])
        for index, (source, target) in enumerate(pairs)
    ]
    for load in loads:
        load.start()

    def across(source, target, send, recv, block):
        return pltpu.make_async_remote_copy(
            src_ref=source,
            dst_ref=target.at[1 - block],
            send_sem=send.at[block],
            recv_sem=recv.at[1 - block],
            device_id={"elem": (left, right)[block]},
            device_id_type=pl.DeviceIdType.MESH,
        )

    def list_copy(index, block):
        source, target = (
            (near_in, near_far),
            (code_in, code_far),
            (count_in, count_far),
        )[index]
        source = source.at[:, block_lanes[block]]
        return across(source, target, list_send.at[index], list_recv.at[index], block)

    def base_copy(block):
        return across(base_pack.at[block], base_far, base_send, base_recv, block)

    def halo_copy(image, block):
        source = (probe_in, first_ref)[image].at[:, :, block_lanes[block]]
        return across(source, halo.at[image], halo_send.at[image], halo_recv.at[image], block)

    def follow_copy(image):
        return arrival(image, (probe_in, first_ref)[image])

    def arrival(image, source=first_ref):
        return pltpu.make_async_remote_copy(
            src_ref=source,
            dst_ref=follow.at[image],
            send_sem=follow_send.at[image],
            recv_sem=follow_recv.at[image],
            device_id={"seg": behind},
            device_id_type=pl.DeviceIdType.MESH,
        )

    pl.semaphore_wait(barrier, 3)
    for index in range(3):
        for block in range(2):
            list_copy(index, block).start()
    for block in range(2):
        halo_copy(0, block).start()

    lane_low = lax.broadcasted_iota(jnp.int32, (NODES, LANES), 1) < HALO
    pack_low = lax.broadcasted_iota(jnp.int32, (96, LANES), 1) < HALO
    list_low = lax.broadcasted_iota(jnp.int32, (SLOTS, LANES), 1) < HALO
    row = lax.broadcasted_iota(jnp.int32, (LANES, LANES), 0)
    slot = lax.broadcasted_iota(jnp.int32, (SLOTS, LANES), 0)
    node = lax.broadcasted_iota(jnp.int32, (NODES, LANES), 0)
    node_at = (
        jnp.right_shift(node, 4),
        jnp.bitwise_and(jnp.right_shift(node, 2), 3),
        jnp.bitwise_and(node, 3),
    )
    trace = lax.broadcasted_iota(jnp.int32, (16, LANES), 0)
    trace_i, trace_j = jnp.right_shift(trace, 2), jnp.bitwise_and(trace, 3)
    blocks = elems * (SHARD // LANES)
    first_block = elem * (SHARD // LANES)

    def one_hot(chosen):
        return jnp.where(row == chosen, 1.0, 0.0).astype(jnp.bfloat16)

    def index_nodes(block, code, live):
        total = jnp.zeros((NODES, LANES), jnp.float32)
        for k in range(SLOTS):
            at = code[k : k + 1]
            way = jnp.right_shift(at, 3)
            end = 3 * jnp.bitwise_and(jnp.right_shift(at, 2), 1)
            turn = jnp.bitwise_and(at, 3)
            far = 3 - end
            place = jnp.where(
                way == 0,
                16 * far + 4 * trace_i + trace_j,
                jnp.where(
                    way == 1,
                    16 * trace_i + 4 * far + trace_j,
                    16 * trace_i + 4 * trace_j + far,
                ),
            )
            places[block, k] = place
            along = jnp.where(way == 0, node_at[0], jnp.where(way == 1, node_at[1], node_at[2]))
            i = jnp.where(way == 0, node_at[1], node_at[0])
            j = jnp.where(way == 2, node_at[1], node_at[2])
            odd = jnp.bitwise_and(turn, 1) == 1
            turned_i, turned_j = jnp.where(odd, j, i), jnp.where(odd, i, j)
            turned_i = jnp.where(turn >= 2, 3 - turned_i, turned_i)
            flip = jnp.logical_or(turn == 1, turn == 2)
            turned_j = jnp.where(flip, 3 - turned_j, turned_j)
            wanted = jnp.where(live[k : k + 1] == 1, end, -1)
            member = along == wanted
            targets[block, k] = jnp.where(member, 4 * turned_i + turned_j, 16)
            total = total + jnp.where(member, 1.0, 0.0)
        own_count[block] = total

    for load in loads[0:3]:
        load.wait()

    def own_lists(block):
        lanes = block_lanes[block]
        near = near_ref[:, lanes]
        used = slot < count_ref[:, lanes]
        place = jnp.where(used, jnp.bitwise_and(near, LANES - 1), -1)
        is_own = jnp.right_shift(near, 7) == first_block + block
        inside, beyond = jnp.where(is_own, place, -1), jnp.where(is_own, -1, place)
        for k in range(SLOTS):
            columns = slice((k % 2) * LANES, (k % 2 + 1) * LANES)
            table[block, k // 2, 0:LANES, columns] = one_hot(inside[k : k + 1])
            table[block, k // 2, LANES:SHARD, columns] = one_hot(beyond[k : k + 1])
        index_nodes(block, code_ref[:, lanes], jnp.where(used, 1, 0))

    def edge_lists():
        near = jnp.where(list_low, near_far[1], near_far[0])
        code = jnp.where(list_low, code_far[1], code_far[0])
        used = slot < jnp.where(list_low[0:1], count_far[1], count_far[0])
        place = jnp.where(used, jnp.bitwise_and(near, LANES - 1), -1)
        outer = jnp.where(
            list_low, lax.rem(first_block + 2, blocks), lax.rem(first_block + blocks - 1, blocks)
        )
        is_outer = jnp.right_shift(near, 7) == outer
        inside, beyond = jnp.where(is_outer, -1, place), jnp.where(is_outer, place, -1)
        to_left, to_right = jnp.where(list_low, -1, beyond), jnp.where(list_low, beyond, -1)
        for k in range(SLOTS):
            columns = slice((k % 2) * LANES, (k % 2 + 1) * LANES)
            for part, chosen in enumerate((inside, to_left, to_right)):
                rows = slice(part * LANES, (part + 1) * LANES)
                edge_table[k // 2, rows, columns] = one_hot(chosen[k : k + 1])
        index_nodes(EDGE, code, jnp.where(used, 1, 0))

    for load in loads[5:7]:
        load.wait()
    for block in range(2):
        packed = base[block].reshape(COMP * NODES, LANES)
        upper, lower = packed[0:96], pltpu.roll(packed[96:192], HALO, 1)
        base_pack[block] = (
            jnp.where(pack_low, upper, lower) if block == 0 else jnp.where(pack_low, lower, upper)
        )
        base_copy(block).start()
    follow_copy(0).start()
    for block in range(2):
        own_lists(block)

    def pieces_of(fields):
        return jnp.concatenate([piece for field in fields for piece in split(field)], axis=0)

    def derivatives(pieces):
        width = 2 * NODES
        beside = jnp.concatenate(
            [pieces[comp * width : (comp + 1) * width] for comp in range(COMP)], axis=1
        )
        return dot(oper_ref[...], jnp.concatenate([beside, beside], axis=0))

    def base_gradient(block):
        grads = derivatives(pieces_of([base[block, comp] for comp in range(COMP)]))
        for comp in range(COMP):
            lanes = slice(comp * LANES, (comp + 1) * LANES)
            for d in range(3):
                base_grad[block, d, comp] = grads[(d + 1) * NODES : (d + 2) * NODES, lanes]

    loads[7].wait()
    for block in range(2):
        base_gradient(block)
    for load in loads[3:5]:
        load.wait()

    def local_terms(block, pieces):
        grads = derivatives(pieces)
        for comp in range(COMP):
            lanes = slice(comp * LANES, (comp + 1) * LANES)
            total = grads[0:NODES, lanes] - own_count[block] * state[block, comp]
            for d in range(3):
                total = total - base[block, d] * grads[(d + 1) * NODES : (d + 2) * NODES, lanes]
            for d in range(3):
                total = total - state[block, d] * base_grad[block, d, comp]
            acc[block, comp] = total

    def add_flux(block, fields, weights):
        for pair in range(SLOTS // 2):
            found = dot(fields, weights(pair))
            for k in (2 * pair, 2 * pair + 1):
                lanes = slice((k % 2) * LANES, (k % 2 + 1) * LANES)
                place = places[block, k]
                target = targets[block, k]
                lookups = jnp.bitwise_and(place, 7)
                origin = jnp.right_shift(place, 3)
                for comp in range(COMP):
                    at = 2 * comp * NODES
                    value = found[at : at + NODES, lanes]
                    value = value + found[at + NODES : at + 2 * NODES, lanes]
                    halves = []
                    for half, choices in enumerate(((0, 1, 2, 3, 6), (4, 5, 6, 7, 1))):
                        rows = slice(8 * half, 8 * half + 8)
                        picked = None
                        for choice in choices:
                            option = jnp.take_along_axis(
                                value[8 * choice : 8 * choice + 8], lookups[rows], axis=0
                            )
                            picked = (
                                option
                                if picked is None
                                else jnp.where(origin[rows] == choice, option, picked)
                            )
                        halves.append(picked)
                    for group in range(8):
                        rows = slice(8 * group, 8 * group + 8)
                        goal = target[rows]
                        spot = jnp.bitwise_and(goal, 7)
                        turned = jnp.where(
                            goal < 8,
                            jnp.take_along_axis(halves[0], spot, axis=0),
                            jnp.take_along_axis(halves[1], spot, axis=0),
                        )
                        acc[block, comp, rows] += jnp.where(goal < 16, turned, 0.0)

    def blend(low, high):
        return [jnp.where(lane_low, low(comp), high(comp)) for comp in range(COMP)]

    def block_field(block):
        return lambda comp: state[block, comp]

    def own_terms(block, carry):
        pieces = pieces_of([state[block, comp] for comp in range(COMP)])
        sources[block, :, 0:LANES] = pieces
        local_terms(block, pieces)
        return carry

    def own_flux(block, carry):
        add_flux(block, sources[block], lambda pair: table[block, pair])
        return carry

    def step_forward(block, carry):
        state[block] = state[block] + TIME_STEP * acc[block]
        return carry

    def one_image(image, carry):
        lax.fori_loop(0, 2, own_terms, 0)
        edge_sources[:, 0:LANES] = pieces_of(blend(block_field(0), block_field(1)))

        @pl.when(image == 0)
        def _():
            for index in range(3):
                for block in range(2):
                    list_copy(index, block).wait_recv()
            edge_lists()

        for side in range(2):
            across(
                state.at[side], halo.at[image], halo_send.at[image], halo_recv.at[image], 1 - side
            ).wait_recv()

        def halo_field(side):
            return lambda comp: halo[image, side, comp]

        sources[0, :, LANES:SHARD] = pieces_of(blend(block_field(1), halo_field(0)))
        sources[1, :, LANES:SHARD] = pieces_of(blend(halo_field(1), block_field(0)))
        for side in range(2):
            lanes = slice((side + 1) * LANES, (side + 2) * LANES)
            edge_sources[:, lanes] = pieces_of([halo[image, side, comp] for comp in range(COMP)])
        lax.fori_loop(0, 2, own_flux, 0)
        edge = blend(halo_field(1), halo_field(0))
        for comp in range(COMP):
            state[EDGE, comp] = edge[comp]

        @pl.when(image == 0)
        def _():
            for block in range(2):
                base_copy(block).wait_recv()
            kept = jnp.where(pack_low, base_far[1], base_far[0])
            other = pltpu.roll(jnp.where(pack_low, base_far[0], base_far[1]), HALO, 1)
            base[EDGE] = jnp.concatenate([kept, other], axis=0).reshape(COMP, NODES, LANES)
            base_gradient(EDGE)

        local_terms(EDGE, pieces_of(edge))
        add_flux(EDGE, edge_sources[...], lambda pair: edge_table[pair])
        lax.fori_loop(0, 3, step_forward, 0)

        lax.fori_loop(0, 2, own_terms, 0)
        sources[0, :, LANES:SHARD] = pieces_of(blend(block_field(1), block_field(EDGE)))
        sources[1, :, LANES:SHARD] = pieces_of(blend(block_field(EDGE), block_field(0)))
        lax.fori_loop(0, 2, own_flux, 0)
        arrival(image).wait_recv()
        for block in range(2):
            lanes = block_lanes[block]
            value = state[block] + TIME_STEP * acc[block] - follow[image, :, :, lanes]
            state[block] = value

            @pl.when(image == 0)
            def _():
                first_ref[:, :, lanes] = value

            @pl.when(image == 1)
            def _():
                second_ref[:, :, lanes] = value

        @pl.when(image == 0)
        def _():
            for block in range(2):
                halo_copy(1, block).start()
            follow_copy(1).start()

        return carry

    lax.fori_loop(0, 2, one_image, 0)
    for block in range(2):
        for index in range(3):
            list_copy(index, block).wait_send()
        base_copy(block).wait_send()
        for image in range(2):
            halo_copy(image, block).wait_send()
    for image in range(2):
        follow_copy(image).wait_send()


def on_device(base_flow, probe_field, neighbours, face_codes, face_counts):
    operators = operator_pieces()
    field = jax.ShapeDtypeStruct((COMP, NODES, SHARD), jnp.float32)
    vmem = pl.BlockSpec(memory_space=pltpu.VMEM)
    first_image, second_image = pl.pallas_call(
        functools.partial(kernel, lax.axis_size("seg"), lax.axis_size("elem")),
        out_shape=(field, field),
        in_specs=[pl.BlockSpec(memory_space=pltpu.HBM)] * 6,
        out_specs=(vmem, vmem),
        scratch_shapes=[
            pltpu.VMEM(operators.shape, jnp.bfloat16),
            pltpu.VMEM((SLOTS, SHARD), jnp.int32),
            pltpu.VMEM((SLOTS, SHARD), jnp.int32),
            pltpu.VMEM((1, SHARD), jnp.int32),
            pltpu.VMEM((2, SLOTS, LANES), jnp.int32),
            pltpu.VMEM((2, SLOTS, LANES), jnp.int32),
            pltpu.VMEM((2, 1, LANES), jnp.int32),
            pltpu.VMEM((3, COMP, NODES, LANES), jnp.float32),
            pltpu.VMEM((2, 96, LANES), jnp.float32),
            pltpu.VMEM((2, 96, LANES), jnp.float32),
            pltpu.VMEM((3, COMP, NODES, LANES), jnp.float32),
            pltpu.VMEM((3, COMP, NODES, LANES), jnp.float32),
            pltpu.VMEM((3, 3, COMP, NODES, LANES), jnp.float32),
            pltpu.VMEM((3, NODES, LANES), jnp.float32),
            pltpu.VMEM((3, SLOTS, 16, LANES), jnp.int32),
            pltpu.VMEM((3, SLOTS, NODES, LANES), jnp.int32),
            pltpu.VMEM((2, SLOTS // 2, SHARD, SHARD), jnp.bfloat16),
            pltpu.VMEM((SLOTS // 2, 3 * LANES, SHARD), jnp.bfloat16),
            pltpu.VMEM((2, 2 * COMP * NODES, SHARD), jnp.bfloat16),
            pltpu.VMEM((2 * COMP * NODES, 3 * LANES), jnp.bfloat16),
            pltpu.VMEM((2, 2, COMP, NODES, LANES), jnp.float32),
            pltpu.VMEM((2, COMP, NODES, SHARD), jnp.float32),
            pltpu.SemaphoreType.DMA((8,)),
            pltpu.SemaphoreType.DMA((3, 2)),
            pltpu.SemaphoreType.DMA((3, 2)),
            pltpu.SemaphoreType.DMA((2,)),
            pltpu.SemaphoreType.DMA((2,)),
            pltpu.SemaphoreType.DMA((2, 2)),
            pltpu.SemaphoreType.DMA((2, 2)),
            pltpu.SemaphoreType.DMA((2,)),
            pltpu.SemaphoreType.DMA((2,)),
        ],
        compiler_params=pltpu.CompilerParams(
            collective_id=0, has_side_effects=True, vmem_limit_bytes=40 * 1024 * 1024
        ),
        name="shooting",
    )(
        *[
            pltpu.with_memory_space_constraint(value, pltpu.HBM)
            for value in (
                base_flow[0],
                probe_field[0],
                neighbours,
                face_codes,
                face_counts.reshape(1, SHARD),
                operators,
            )
        ]
    )
    return (first_image[None], second_image[None])


def solution(mesh):
    placed = (
        P("seg", None, None, "elem"),
        P("seg", None, None, "elem"),
        P(None, "elem"),
        P(None, "elem"),
        P("elem"),
    )
    return jax.shard_map(
        on_device,
        mesh=mesh,
        in_specs=placed,
        out_specs=(P("seg", None, None, "elem"), P("seg", None, None, "elem")),
        check_vma=False,
    )
```

```python
import functools

import jax
import jax.numpy as jnp
import ml_dtypes
import numpy as np
from jax import lax
from jax.experimental import pallas as pl
from jax.experimental.pallas import tpu as pltpu
from jax.sharding import PartitionSpec as P

STEPS = 2
VISCOSITY = 0.05
PENALTY = 1.0
TIME_STEP = 0.05

COMP = 3
NODES = 64
SHARD = 256
LANES = 128
HALO = 64
MIDDLE, SIDES, EDGE, OUTER = 0, 1, 2, 3
SLOTS = 6


def operator_tables():
    points = np.array([-1.0, -1.0 / np.sqrt(5.0), 1.0 / np.sqrt(5.0), 1.0])
    barycentric = np.array(
        [
            1.0 / np.prod([points[row] - points[col] for col in range(4) if col != row])
            for row in range(4)
        ]
    )
    derivative = np.zeros((4, 4))
    for row in range(4):
        for col in range(4):
            if row != col:
                derivative[row, col] = (
                    barycentric[col] / barycentric[row] / (points[row] - points[col])
                )
        derivative[row, row] = -np.sum(derivative[row])
    identity = np.eye(4)
    gradient = [
        np.kron(np.kron(derivative, identity), identity),
        np.kron(np.kron(identity, derivative), identity),
        np.kron(np.kron(identity, identity), derivative),
    ]
    laplacian = sum(table @ table for table in gradient)
    return gradient, laplacian


def operator_pieces():
    gradient, laplacian = operator_tables()
    stacked = np.concatenate([VISCOSITY * laplacian] + gradient, axis=0)
    high = stacked.astype(ml_dtypes.bfloat16)
    low = (stacked - high.astype(np.float64)).astype(ml_dtypes.bfloat16)
    return jnp.asarray(np.concatenate([high, high, low, low], axis=1))


def split(value):
    high = value.astype(jnp.bfloat16)
    low = (value - high.astype(jnp.float32)).astype(jnp.bfloat16)
    return high, low


def dot(left, right):
    return jnp.dot(left, right, preferred_element_type=jnp.float32)


def kernel(
    segs,
    elems,
    base_in,
    probe_in,
    near_in,
    code_in,
    count_in,
    oper_in,
    first_ref,
    second_ref,
    oper_ref,
    near_ref,
    code_ref,
    count_ref,
    near_far,
    code_far,
    count_far,
    loaded,
    base,
    base_pack,
    base_far,
    state,
    acc,
    base_grad,
    own_count,
    places,
    turns,
    faces,
    table,
    sources,
    gathered,
    halo,
    follow,
    input_sem,
    list_send,
    list_recv,
    base_send,
    base_recv,
    halo_send,
    halo_recv,
    follow_send,
    follow_recv,
):
    seg = lax.axis_index("seg")
    elem = lax.axis_index("elem")
    right = lax.rem(elem + 1, elems)
    left = lax.rem(elem + elems - 1, elems)
    ahead = lax.rem(seg + 1, segs)
    behind = lax.rem(seg + segs - 1, segs)
    barrier = pltpu.get_barrier_semaphore()
    for target in ({"elem": left}, {"elem": right}, {"seg": ahead}):
        pl.semaphore_signal(
            barrier, inc=1, device_id=target, device_id_type=pl.DeviceIdType.MESH
        )
    block_lanes = (slice(0, LANES), slice(LANES, SHARD))
    pairs = [(near_in, near_ref), (code_in, code_ref), (count_in, count_ref)]
    for block in range(2):
        pairs.append((probe_in.at[:, :, block_lanes[block]], loaded.at[0, block]))
    for block in range(2):
        pairs.append((base_in.at[:, :, block_lanes[block]], loaded.at[1, block]))
    pairs.append((oper_in, oper_ref))
    loads = [
        pltpu.make_async_copy(source, target, input_sem.at[index])
        for index, (source, target) in enumerate(pairs)
    ]
    for load in loads:
        load.start()

    def across(source, target, send, recv, block):
        return pltpu.make_async_remote_copy(
            src_ref=source,
            dst_ref=target.at[1 - block],
            send_sem=send.at[block],
            recv_sem=recv.at[1 - block],
            device_id={"elem": (left, right)[block]},
            device_id_type=pl.DeviceIdType.MESH,
        )

    def list_copy(index, block):
        source, target = (
            (near_in, near_far),
            (code_in, code_far),
            (count_in, count_far),
        )[index]
        source = source.at[:, block_lanes[block]]
        return across(source, target, list_send.at[index], list_recv.at[index], block)

    def base_copy(block):
        return across(base_pack.at[block], base_far, base_send, base_recv, block)

    def halo_copy(image, block):
        source = (probe_in, first_ref)[image].at[:, :, block_lanes[block]]
        return across(source, halo.at[image], halo_send.at[image], halo_recv.at[image], block)

    def follow_copy(image):
        return arrival(image, (probe_in, first_ref)[image])

    def arrival(image, source=first_ref):
        return pltpu.make_async_remote_copy(
            src_ref=source,
            dst_ref=follow.at[image],
            send_sem=follow_send.at[image],
            recv_sem=follow_recv.at[image],
            device_id={"seg": behind},
            device_id_type=pl.DeviceIdType.MESH,
        )

    pl.semaphore_wait(barrier, 3)
    for index in range(3):
        for block in range(2):
            list_copy(index, block).start()
    for block in range(2):
        halo_copy(0, block).start()

    lane_low = lax.broadcasted_iota(jnp.int32, (NODES, LANES), 1) < HALO
    pack_low = lax.broadcasted_iota(jnp.int32, (96, LANES), 1) < HALO
    list_low = lax.broadcasted_iota(jnp.int32, (SLOTS, LANES), 1) < HALO
    count_low = lax.broadcasted_iota(jnp.int32, (1, LANES), 1) < HALO
    row = lax.broadcasted_iota(jnp.int32, (LANES, LANES), 0)
    slot = lax.broadcasted_iota(jnp.int32, (SLOTS, LANES), 0)
    node = lax.broadcasted_iota(jnp.int32, (NODES, LANES), 0)
    node_at = (
        jnp.right_shift(node, 4),
        jnp.bitwise_and(jnp.right_shift(node, 2), 3),
        jnp.bitwise_and(node, 3),
    )
    trace = lax.broadcasted_iota(jnp.int32, (16, LANES), 0)
    trace_i, trace_j = jnp.right_shift(trace, 2), jnp.bitwise_and(trace, 3)
    sublane = lax.broadcasted_iota(jnp.int32, (8, LANES), 0)
    blocks = elems * (SHARD // LANES)
    block_a = elem * (SHARD // LANES)
    before_a = lax.rem(block_a + blocks - 1, blocks)
    after_b = lax.rem(block_a + 2, blocks)

    def index_block(block, near, code, count):
        used = slot < count
        lane = jnp.bitwise_and(near, LANES - 1)
        origin = jnp.right_shift(near, 7)
        high = lane >= HALO
        in_a, in_b = origin == block_a, origin == block_a + 1
        back = origin == before_a
        own = jnp.logical_or(in_a, in_b)
        middle = jnp.logical_and(own, in_a == high)
        outer = jnp.logical_and(jnp.logical_not(own), back != high)
        kind = jnp.where(own, jnp.where(middle, MIDDLE, SIDES), jnp.where(outer, OUTER, EDGE))
        kind = jnp.where(used, kind, -1)
        first = 1 if block == EDGE else 0
        for part in range(2 if block == MIDDLE else 3):
            chosen = jnp.where(kind == first + part, lane, -1)
            rows = slice(part * LANES, (part + 1) * LANES)
            for k in range(SLOTS):
                columns = slice((k % 2) * LANES, (k % 2 + 1) * LANES)
                table[block, k // 2, rows, columns] = jnp.where(
                    row == chosen[k : k + 1], 1.0, 0.0
                ).astype(jnp.bfloat16)
        way = jnp.right_shift(code, 3)
        far = 3 - 3 * jnp.bitwise_and(jnp.right_shift(code, 2), 1)
        turn = jnp.bitwise_and(code, 3)
        face = jnp.right_shift(code, 2)
        total = jnp.zeros((NODES, LANES), jnp.float32)
        for which in range(6):
            hits = jnp.where(jnp.logical_and(face == which, used), 1.0, 0.0)
            on_face = node_at[which // 2] == 3 * (which % 2)
            total = total + jnp.where(on_face, jnp.sum(hits, axis=0, keepdims=True), 0.0)
        own_count[block] = total
        for k in range(SLOTS):
            row_way, row_far, row_turn = way[k : k + 1], far[k : k + 1], turn[k : k + 1]
            places[block, k] = jnp.where(
                row_way == 0,
                16 * row_far + 4 * trace_i + trace_j,
                jnp.where(
                    row_way == 1,
                    16 * trace_i + 4 * row_far + trace_j,
                    16 * trace_i + 4 * trace_j + row_far,
                ),
            )
            odd = jnp.bitwise_and(row_turn, 1) == 1
            turned_i = jnp.where(odd, trace_j, trace_i)
            turned_j = jnp.where(odd, trace_i, trace_j)
            turned_i = jnp.where(row_turn >= 2, 3 - turned_i, turned_i)
            flip = jnp.logical_or(row_turn == 1, row_turn == 2)
            turned_j = jnp.where(flip, 3 - turned_j, turned_j)
            turns[block, k] = 4 * turned_i + turned_j
            faces[block, k] = jnp.broadcast_to(face[k : k + 1], (8, LANES))

    def pieces_of(fields):
        return jnp.concatenate([piece for field in fields for piece in split(field)], axis=0)

    def derivatives(pieces):
        width = 2 * NODES
        beside = jnp.concatenate(
            [pieces[comp * width : (comp + 1) * width] for comp in range(COMP)], axis=1
        )
        return dot(oper_ref[...], jnp.concatenate([beside, beside], axis=0))

    def base_gradient(block):
        grads = derivatives(pieces_of([base[block, comp] for comp in range(COMP)]))
        for comp in range(COMP):
            lanes = slice(comp * LANES, (comp + 1) * LANES)
            for d in range(3):
                base_grad[block, d, comp] = grads[(d + 1) * NODES : (d + 2) * NODES, lanes]

    for load in loads[5:7]:
        load.wait()
    for block in range(2):
        packed = loaded[1, block].reshape(COMP * NODES, LANES)
        upper, lower = packed[0:96], pltpu.roll(packed[96:192], HALO, 1)
        base_pack[block] = (
            jnp.where(pack_low, upper, lower) if block == 0 else jnp.where(pack_low, lower, upper)
        )
        base_copy(block).start()
    follow_copy(0).start()
    for load in loads[0:5]:
        load.wait()
    for comp in range(COMP):
        for target, kind in ((state, 0), (base, 1)):
            in_a, in_b = loaded[kind, 0, comp], loaded[kind, 1, comp]
            target[MIDDLE, comp] = jnp.where(lane_low, in_b, in_a)
            target[SIDES, comp] = jnp.where(lane_low, in_a, in_b)
    for block in (MIDDLE, SIDES):
        lists = []
        for ref, low in ((near_ref, list_low), (code_ref, list_low), (count_ref, count_low)):
            in_a, in_b = ref[:, 0:LANES], ref[:, LANES:SHARD]
            if block == MIDDLE:
                in_a, in_b = in_b, in_a
            lists.append(jnp.where(low, in_a, in_b))
        index_block(block, *lists)
    loads[7].wait()
    for block in (MIDDLE, SIDES):
        base_gradient(block)

    def local_terms(block, pieces, started):
        grads = derivatives(pieces)
        for comp in range(COMP):
            lanes = slice(comp * LANES, (comp + 1) * LANES)
            total = grads[0:NODES, lanes] - own_count[block] * state[block, comp]
            for d in range(3):
                total = total - base[block, d] * grads[(d + 1) * NODES : (d + 2) * NODES, lanes]
            for d in range(3):
                total = total - state[block, d] * base_grad[block, d, comp]
            acc[block, comp] = total + acc[block, comp] if started else total

    def add_flux(block, fields, depth):
        for pair in range(SLOTS // 2):
            found = dot(fields, table[block, pair, 0:depth])
            for comp in range(COMP):
                at = 2 * comp * NODES
                value = found[at : at + NODES] + found[at + NODES : at + 2 * NODES]
                gathered[2 * pair, comp] = value[:, 0:LANES]
                gathered[2 * pair + 1, comp] = value[:, LANES:SHARD]

        def component(comp, carry):
            sums = [[None, None] for _ in range(6)]
            for k in range(SLOTS):
                halves = []
                for half, choices in enumerate(((0, 1, 2, 3, 6), (4, 5, 6, 7, 1))):
                    place = places[block, k, 8 * half : 8 * half + 8]
                    lookup = jnp.bitwise_and(place, 7)
                    origin = jnp.right_shift(place, 3)
                    picked = None
                    for choice in choices:
                        option = jnp.take_along_axis(
                            gathered[k, comp, 8 * choice : 8 * choice + 8], lookup, axis=0
                        )
                        picked = (
                            option
                            if picked is None
                            else jnp.where(origin == choice, option, picked)
                        )
                    halves.append(picked)
                for half in range(2):
                    goal = turns[block, k, 8 * half : 8 * half + 8]
                    spot = jnp.bitwise_and(goal, 7)
                    turned = jnp.where(
                        goal < 8,
                        jnp.take_along_axis(halves[0], spot, axis=0),
                        jnp.take_along_axis(halves[1], spot, axis=0),
                    )
                    for which in range(6):
                        term = jnp.where(faces[block, k] == which, turned, 0.0)
                        held = sums[which][half]
                        sums[which][half] = term if held is None else held + term
            swapped = jnp.bitwise_xor(sublane, 4)
            edge_of = jnp.bitwise_and(sublane, 3)
            for group in range(8):
                half, odd_a = group // 4, (group // 2) % 2
                rows = slice(8 * group, 8 * group + 8)
                total = acc[block, comp, rows]
                if group < 2:
                    total = total + sums[0][group]
                if group >= 6:
                    total = total + sums[1][group - 6]
                side = sums[2 + group % 2][half]
                if odd_a != group % 2:
                    side = jnp.take_along_axis(side, swapped, axis=0)
                total = total + jnp.where((sublane < 4) == (group % 2 == 0), side, 0.0)
                spot = 2 * (group % 4) + jnp.right_shift(sublane, 2)
                front = jnp.take_along_axis(sums[4][half], spot, axis=0)
                rear = jnp.take_along_axis(sums[5][half], spot, axis=0)
                total = total + jnp.where(edge_of == 0, front, jnp.where(edge_of == 3, rear, 0.0))
                acc[block, comp, rows] = total
            return carry

        lax.fori_loop(0, COMP, component, 0)

    def blend(low, high):
        return [jnp.where(lane_low, low[comp], high[comp]) for comp in range(COMP)]

    def own_terms(block, carry):
        pieces = pieces_of([state[block, comp] for comp in range(COMP)])
        sources[block] = pieces
        local_terms(block, pieces, False)
        return carry

    def wide_flux(block, carry):
        fields = jnp.concatenate([sources[block - 1 + part] for part in range(3)], axis=1)
        add_flux(block, fields, 3 * LANES)
        return carry

    def step_forward(block, carry):
        state[block] = state[block] + TIME_STEP * acc[block]
        return carry

    def one_step(step, carry):
        image, odd = step // STEPS, step % STEPS
        lax.fori_loop(MIDDLE, EDGE, own_terms, 0)
        fields = jnp.concatenate([sources[MIDDLE], sources[SIDES]], axis=1)
        add_flux(MIDDLE, fields, SHARD)

        @pl.when(step == 0)
        def _():
            for index in range(3):
                for block in range(2):
                    list_copy(index, block).wait_recv()
            index_block(
                EDGE,
                jnp.where(list_low, near_far[1], near_far[0]),
                jnp.where(list_low, code_far[1], code_far[0]),
                jnp.where(count_low, count_far[1], count_far[0]),
            )

        @pl.when(odd == 0)
        def _():
            for side in range(2):
                across(
                    loaded.at[0, side],
                    halo.at[image],
                    halo_send.at[image],
                    halo_recv.at[image],
                    1 - side,
                ).wait_recv()
            from_left = [halo[image, 0, comp] for comp in range(COMP)]
            from_right = [halo[image, 1, comp] for comp in range(COMP)]
            edge = blend(from_right, from_left)
            for comp in range(COMP):
                state[EDGE, comp] = edge[comp]
            sources[OUTER] = pieces_of(blend(from_left, from_right))
            acc[EDGE] = jnp.zeros((COMP, NODES, LANES), jnp.float32)

        sources[EDGE] = pieces_of([state[EDGE, comp] for comp in range(COMP)])
        done = EDGE + 1 - odd
        lax.fori_loop(SIDES, done, wide_flux, 0)

        @pl.when(step == 0)
        def _():
            for block in range(2):
                base_copy(block).wait_recv()
            kept = jnp.where(pack_low, base_far[1], base_far[0])
            other = pltpu.roll(jnp.where(pack_low, base_far[0], base_far[1]), HALO, 1)
            base[EDGE] = jnp.concatenate([kept, other], axis=0).reshape(COMP, NODES, LANES)
            base_gradient(EDGE)

        @pl.when(odd == 0)
        def _():
            local_terms(EDGE, sources[EDGE], True)

        lax.fori_loop(MIDDLE, done, step_forward, 0)

        @pl.when(odd == 1)
        def _():
            arrival(image).wait_recv()
            for comp in range(COMP):
                middle, sides = state[MIDDLE, comp], state[SIDES, comp]
                in_a = jnp.where(lane_low, sides, middle) - follow[image, comp, :, 0:LANES]
                in_b = jnp.where(lane_low, middle, sides) - follow[image, comp, :, LANES:SHARD]

                @pl.when(image == 0)
                def _():
                    first_ref[comp, :, 0:LANES] = in_a
                    first_ref[comp, :, LANES:SHARD] = in_b
                    state[MIDDLE, comp] = jnp.where(lane_low, in_b, in_a)
                    state[SIDES, comp] = jnp.where(lane_low, in_a, in_b)

                @pl.when(image == 1)
                def _():
                    second_ref[comp, :, 0:LANES] = in_a
                    second_ref[comp, :, LANES:SHARD] = in_b

        @pl.when(step == STEPS - 1)
        def _():
            for block in range(2):
                halo_copy(1, block).start()
            follow_copy(1).start()

        return carry

    lax.fori_loop(0, 2 * STEPS, one_step, 0)
    for block in range(2):
        for index in range(3):
            list_copy(index, block).wait_send()
        base_copy(block).wait_send()
        for image in range(2):
            halo_copy(image, block).wait_send()
    for image in range(2):
        follow_copy(image).wait_send()


def on_device(base_flow, probe_field, neighbours, face_codes, face_counts):
    operators = operator_pieces()
    field = jax.ShapeDtypeStruct((COMP, NODES, SHARD), jnp.float32)
    vmem = pl.BlockSpec(memory_space=pltpu.VMEM)
    first_image, second_image = pl.pallas_call(
        functools.partial(kernel, lax.axis_size("seg"), lax.axis_size("elem")),
        out_shape=(field, field),
        in_specs=[pl.BlockSpec(memory_space=pltpu.HBM)] * 6,
        out_specs=(vmem, vmem),
        scratch_shapes=[
            pltpu.VMEM(operators.shape, jnp.bfloat16),
            pltpu.VMEM((SLOTS, SHARD), jnp.int32),
            pltpu.VMEM((SLOTS, SHARD), jnp.int32),
            pltpu.VMEM((1, SHARD), jnp.int32),
            pltpu.VMEM((2, SLOTS, LANES), jnp.int32),
            pltpu.VMEM((2, SLOTS, LANES), jnp.int32),
            pltpu.VMEM((2, 1, LANES), jnp.int32),
            pltpu.VMEM((2, 2, COMP, NODES, LANES), jnp.float32),
            pltpu.VMEM((3, COMP, NODES, LANES), jnp.float32),
            pltpu.VMEM((2, 96, LANES), jnp.float32),
            pltpu.VMEM((2, 96, LANES), jnp.float32),
            pltpu.VMEM((3, COMP, NODES, LANES), jnp.float32),
            pltpu.VMEM((3, COMP, NODES, LANES), jnp.float32),
            pltpu.VMEM((3, 3, COMP, NODES, LANES), jnp.float32),
            pltpu.VMEM((3, NODES, LANES), jnp.float32),
            pltpu.VMEM((3, SLOTS, 16, LANES), jnp.int32),
            pltpu.VMEM((3, SLOTS, 16, LANES), jnp.int32),
            pltpu.VMEM((3, SLOTS, 8, LANES), jnp.int32),
            pltpu.VMEM((3, SLOTS // 2, 3 * LANES, SHARD), jnp.bfloat16),
            pltpu.VMEM((4, 2 * COMP * NODES, LANES), jnp.bfloat16),
            pltpu.VMEM((SLOTS, COMP, NODES, LANES), jnp.float32),
            pltpu.VMEM((2, 2, COMP, NODES, LANES), jnp.float32),
            pltpu.VMEM((2, COMP, NODES, SHARD), jnp.float32),
            pltpu.SemaphoreType.DMA((8,)),
            pltpu.SemaphoreType.DMA((3, 2)),
            pltpu.SemaphoreType.DMA((3, 2)),
            pltpu.SemaphoreType.DMA((2,)),
            pltpu.SemaphoreType.DMA((2,)),
            pltpu.SemaphoreType.DMA((2, 2)),
            pltpu.SemaphoreType.DMA((2, 2)),
            pltpu.SemaphoreType.DMA((2,)),
            pltpu.SemaphoreType.DMA((2,)),
        ],
        compiler_params=pltpu.CompilerParams(
            collective_id=0, has_side_effects=True, vmem_limit_bytes=40 * 1024 * 1024
        ),
        name="shooting",
    )(
        *[
            pltpu.with_memory_space_constraint(value, pltpu.HBM)
            for value in (
                base_flow[0],
                probe_field[0],
                neighbours,
                face_codes,
                face_counts.reshape(1, SHARD),
                operators,
            )
        ]
    )
    return (first_image[None], second_image[None])


def solution(mesh):
    placed = (
        P("seg", None, None, "elem"),
        P("seg", None, None, "elem"),
        P(None, "elem"),
        P(None, "elem"),
        P("elem"),
    )
    return jax.shard_map(
        on_device,
        mesh=mesh,
        in_specs=placed,
        out_specs=(P("seg", None, None, "elem"), P("seg", None, None, "elem")),
        check_vma=False,
    )
```

```python
import functools

import jax
import jax.numpy as jnp
import ml_dtypes
import numpy as np
from jax import lax
from jax.experimental import pallas as pl
from jax.experimental.pallas import tpu as pltpu
from jax.sharding import PartitionSpec as P

STEPS = 2
VISCOSITY = 0.05
PENALTY = 1.0
TIME_STEP = 0.05

COMP = 3
NODES = 64
SHARD = 256
LANES = 128
HALO = 64
EDGE = 2
SLOTS = 6


def operator_tables():
    points = np.array([-1.0, -1.0 / np.sqrt(5.0), 1.0 / np.sqrt(5.0), 1.0])
    barycentric = np.array(
        [
            1.0 / np.prod([points[row] - points[col] for col in range(4) if col != row])
            for row in range(4)
        ]
    )
    derivative = np.zeros((4, 4))
    for row in range(4):
        for col in range(4):
            if row != col:
                derivative[row, col] = (
                    barycentric[col] / barycentric[row] / (points[row] - points[col])
                )
        derivative[row, row] = -np.sum(derivative[row])
    identity = np.eye(4)
    gradient = [
        np.kron(np.kron(derivative, identity), identity),
        np.kron(np.kron(identity, derivative), identity),
        np.kron(np.kron(identity, identity), derivative),
    ]
    laplacian = sum(table @ table for table in gradient)
    return gradient, laplacian


def operator_pieces():
    gradient, laplacian = operator_tables()
    stacked = np.concatenate([VISCOSITY * laplacian] + gradient, axis=0)
    high = stacked.astype(ml_dtypes.bfloat16)
    low = (stacked - high.astype(np.float64)).astype(ml_dtypes.bfloat16)
    return jnp.asarray(np.concatenate([high, high, low, low], axis=1))


def split(value):
    high = value.astype(jnp.bfloat16)
    low = (value - high.astype(jnp.float32)).astype(jnp.bfloat16)
    return high, low


def dot(left, right):
    return jnp.dot(left, right, preferred_element_type=jnp.float32)


def kernel(
    segs,
    elems,
    base_in,
    probe_in,
    near_in,
    code_in,
    count_in,
    oper_in,
    first_ref,
    second_ref,
    oper_ref,
    near_ref,
    code_ref,
    count_ref,
    near_far,
    code_far,
    count_far,
    base,
    base_pack,
    base_far,
    state,
    acc,
    base_grad,
    own_count,
    places,
    targets,
    table,
    edge_table,
    sources,
    edge_sources,
    halo,
    follow,
    input_sem,
    list_send,
    list_recv,
    base_send,
    base_recv,
    halo_send,
    halo_recv,
    follow_send,
    follow_recv,
):
    seg = lax.axis_index("seg")
    elem = lax.axis_index("elem")
    right = lax.rem(elem + 1, elems)
    left = lax.rem(elem + elems - 1, elems)
    ahead = lax.rem(seg + 1, segs)
    behind = lax.rem(seg + segs - 1, segs)
    barrier = pltpu.get_barrier_semaphore()
    for target in ({"elem": left}, {"elem": right}, {"seg": ahead}):
        pl.semaphore_signal(
            barrier, inc=1, device_id=target, device_id_type=pl.DeviceIdType.MESH
        )
    block_lanes = (slice(0, LANES), slice(LANES, SHARD))
    pairs = [(near_in, near_ref), (code_in, code_ref), (count_in, count_ref)]
    for block in range(2):
        pairs.append((probe_in.at[:, :, block_lanes[block]], state.at[block]))
    for block in range(2):
        pairs.append((base_in.at[:, :, block_lanes[block]], base.at[block]))
    pairs.append((oper_in, oper_ref))
    loads = [
        pltpu.make_async_copy(source, target, input_sem.at[index])
        for index, (source, target) in enumerate(pairs)
    ]
    for load in loads:
        load.start()

    def across(source, target, send, recv, block):
        return pltpu.make_async_remote_copy(
            src_ref=source,
            dst_ref=target.at[1 - block],
            send_sem=send.at[block],
            recv_sem=recv.at[1 - block],
            device_id={"elem": (left, right)[block]},
            device_id_type=pl.DeviceIdType.MESH,
        )

    def list_copy(index, block):
        source, target = (
            (near_in, near_far),
            (code_in, code_far),
            (count_in, count_far),
        )[index]
        source = source.at[:, block_lanes[block]]
        return across(source, target, list_send.at[index], list_recv.at[index], block)

    def base_copy(block):
        return across(base_pack.at[block], base_far, base_send, base_recv, block)

    def halo_copy(image, block):
        source = (probe_in, first_ref)[image].at[:, :, block_lanes[block]]
        return across(source, halo.at[image], halo_send.at[image], halo_recv.at[image], block)

    def follow_copy(image):
        return arrival(image, (probe_in, first_ref)[image])

    def arrival(image, source=first_ref):
        return pltpu.make_async_remote_copy(
            src_ref=source,
            dst_ref=follow.at[image],
            send_sem=follow_send.at[image],
            recv_sem=follow_recv.at[image],
            device_id={"seg": behind},
            device_id_type=pl.DeviceIdType.MESH,
        )

    pl.semaphore_wait(barrier, 3)
    for index in range(3):
        for block in range(2):
            list_copy(index, block).start()
    for block in range(2):
        halo_copy(0, block).start()

    lane_low = lax.broadcasted_iota(jnp.int32, (NODES, LANES), 1) < HALO
    pack_low = lax.broadcasted_iota(jnp.int32, (96, LANES), 1) < HALO
    list_low = lax.broadcasted_iota(jnp.int32, (SLOTS, LANES), 1) < HALO
    row = lax.broadcasted_iota(jnp.int32, (LANES, LANES), 0)
    slot = lax.broadcasted_iota(jnp.int32, (SLOTS, LANES), 0)
    node = lax.broadcasted_iota(jnp.int32, (NODES, LANES), 0)
    node_at = (
        jnp.right_shift(node, 4),
        jnp.bitwise_and(jnp.right_shift(node, 2), 3),
        jnp.bitwise_and(node, 3),
    )
    trace = lax.broadcasted_iota(jnp.int32, (16, LANES), 0)
    trace_i, trace_j = jnp.right_shift(trace, 2), jnp.bitwise_and(trace, 3)
    blocks = elems * (SHARD // LANES)
    first_block = elem * (SHARD // LANES)

    def one_hot(chosen):
        return jnp.where(row == chosen, 1.0, 0.0).astype(jnp.bfloat16)

    def index_nodes(block, code, live):
        total = jnp.zeros((NODES, LANES), jnp.float32)
        for k in range(SLOTS):
            at = code[k : k + 1]
            way = jnp.right_shift(at, 3)
            end = 3 * jnp.bitwise_and(jnp.right_shift(at, 2), 1)
            turn = jnp.bitwise_and(at, 3)
            far = 3 - end
            place = jnp.where(
                way == 0,
                16 * far + 4 * trace_i + trace_j,
                jnp.where(
                    way == 1,
                    16 * trace_i + 4 * far + trace_j,
                    16 * trace_i + 4 * trace_j + far,
                ),
            )
            places[block, k] = place
            along = jnp.where(way == 0, node_at[0], jnp.where(way == 1, node_at[1], node_at[2]))
            i = jnp.where(way == 0, node_at[1], node_at[0])
            j = jnp.where(way == 2, node_at[1], node_at[2])
            odd = jnp.bitwise_and(turn, 1) == 1
            turned_i, turned_j = jnp.where(odd, j, i), jnp.where(odd, i, j)
            turned_i = jnp.where(turn >= 2, 3 - turned_i, turned_i)
            flip = jnp.logical_or(turn == 1, turn == 2)
            turned_j = jnp.where(flip, 3 - turned_j, turned_j)
            wanted = jnp.where(live[k : k + 1] == 1, end, -1)
            member = along == wanted
            targets[block, k] = jnp.where(member, 4 * turned_i + turned_j, 16)
            total = total + jnp.where(member, 1.0, 0.0)
        own_count[block] = total

    for load in loads[0:3]:
        load.wait()

    def own_lists(block):
        lanes = block_lanes[block]
        near = near_ref[:, lanes]
        used = slot < count_ref[:, lanes]
        place = jnp.where(used, jnp.bitwise_and(near, LANES - 1), -1)
        is_own = jnp.right_shift(near, 7) == first_block + block
        inside, beyond = jnp.where(is_own, place, -1), jnp.where(is_own, -1, place)
        for k in range(SLOTS):
            columns = slice((k % 2) * LANES, (k % 2 + 1) * LANES)
            table[block, k // 2, 0:LANES, columns] = one_hot(inside[k : k + 1])
            table[block, k // 2, LANES:SHARD, columns] = one_hot(beyond[k : k + 1])
        index_nodes(block, code_ref[:, lanes], jnp.where(used, 1, 0))

    def edge_lists():
        near = jnp.where(list_low, near_far[1], near_far[0])
        code = jnp.where(list_low, code_far[1], code_far[0])
        used = slot < jnp.where(list_low[0:1], count_far[1], count_far[0])
        place = jnp.where(used, jnp.bitwise_and(near, LANES - 1), -1)
        outer = jnp.where(
            list_low, lax.rem(first_block + 2, blocks), lax.rem(first_block + blocks - 1, blocks)
        )
        is_outer = jnp.right_shift(near, 7) == outer
        inside, beyond = jnp.where(is_outer, -1, place), jnp.where(is_outer, place, -1)
        to_left, to_right = jnp.where(list_low, -1, beyond), jnp.where(list_low, beyond, -1)
        for k in range(SLOTS):
            columns = slice((k % 2) * LANES, (k % 2 + 1) * LANES)
            for part, chosen in enumerate((inside, to_left, to_right)):
                rows = slice(part * LANES, (part + 1) * LANES)
                edge_table[k // 2, rows, columns] = one_hot(chosen[k : k + 1])
        index_nodes(EDGE, code, jnp.where(used, 1, 0))

    for load in loads[5:7]:
        load.wait()
    for block in range(2):
        packed = base[block].reshape(COMP * NODES, LANES)
        upper, lower = packed[0:96], pltpu.roll(packed[96:192], HALO, 1)
        base_pack[block] = (
            jnp.where(pack_low, upper, lower) if block == 0 else jnp.where(pack_low, lower, upper)
        )
        base_copy(block).start()
    follow_copy(0).start()
    for block in range(2):
        own_lists(block)

    def pieces_of(fields):
        return jnp.concatenate([piece for field in fields for piece in split(field)], axis=0)

    def derivatives(pieces):
        width = 2 * NODES
        beside = jnp.concatenate(
            [pieces[comp * width : (comp + 1) * width] for comp in range(COMP)], axis=1
        )
        return dot(oper_ref[...], jnp.concatenate([beside, beside], axis=0))

    def base_gradient(block):
        grads = derivatives(pieces_of([base[block, comp] for comp in range(COMP)]))
        for comp in range(COMP):
            lanes = slice(comp * LANES, (comp + 1) * LANES)
            for d in range(3):
                base_grad[block, d, comp] = grads[(d + 1) * NODES : (d + 2) * NODES, lanes]

    loads[7].wait()
    for block in range(2):
        base_gradient(block)
    for load in loads[3:5]:
        load.wait()

    def local_terms(block, pieces):
        grads = derivatives(pieces)
        for comp in range(COMP):
            lanes = slice(comp * LANES, (comp + 1) * LANES)
            total = grads[0:NODES, lanes] - own_count[block] * state[block, comp]
            for d in range(3):
                total = total - base[block, d] * grads[(d + 1) * NODES : (d + 2) * NODES, lanes]
            for d in range(3):
                total = total - state[block, d] * base_grad[block, d, comp]
            acc[block, comp] = total

    def add_flux(block, fields, weights):
        for pair in range(SLOTS // 2):
            found = dot(fields, weights(pair))
            for k in (2 * pair, 2 * pair + 1):
                lanes = slice((k % 2) * LANES, (k % 2 + 1) * LANES)
                place = places[block, k]
                target = targets[block, k]
                lookups = jnp.bitwise_and(place, 7)
                origin = jnp.right_shift(place, 3)
                for comp in range(COMP):
                    at = 2 * comp * NODES
                    value = found[at : at + NODES, lanes]
                    value = value + found[at + NODES : at + 2 * NODES, lanes]
                    halves = []
                    for half, choices in enumerate(((0, 1, 2, 3, 6), (4, 5, 6, 7, 1))):
                        rows = slice(8 * half, 8 * half + 8)
                        picked = None
                        for choice in choices:
                            option = jnp.take_along_axis(
                                value[8 * choice : 8 * choice + 8], lookups[rows], axis=0
                            )
                            picked = (
                                option
                                if picked is None
                                else jnp.where(origin[rows] == choice, option, picked)
                            )
                        halves.append(picked)
                    for group in range(8):
                        rows = slice(8 * group, 8 * group + 8)
                        goal = target[rows]
                        spot = jnp.bitwise_and(goal, 7)
                        turned = jnp.where(
                            goal < 8,
                            jnp.take_along_axis(halves[0], spot, axis=0),
                            jnp.take_along_axis(halves[1], spot, axis=0),
                        )
                        acc[block, comp, rows] += jnp.where(goal < 16, turned, 0.0)

    def blend(low, high):
        return [jnp.where(lane_low, low(comp), high(comp)) for comp in range(COMP)]

    def block_field(block):
        return lambda comp: state[block, comp]

    def own_terms(block):
        pieces = pieces_of([state[block, comp] for comp in range(COMP)])
        sources[block, :, 0:LANES] = pieces
        local_terms(block, pieces)

    def own_flux(block):
        add_flux(block, sources[block], lambda pair: table[block, pair])

    def one_image(image):
        for block in range(2):
            own_terms(block)
        edge_sources[:, 0:LANES] = pieces_of(blend(block_field(0), block_field(1)))

        if image == 0:
            for index in range(3):
                for block in range(2):
                    list_copy(index, block).wait_recv()
            edge_lists()

        for side in range(2):
            across(
                state.at[side], halo.at[image], halo_send.at[image], halo_recv.at[image], 1 - side
            ).wait_recv()

        def halo_field(side):
            return lambda comp: halo[image, side, comp]

        sources[0, :, LANES:SHARD] = pieces_of(blend(block_field(1), halo_field(0)))
        sources[1, :, LANES:SHARD] = pieces_of(blend(halo_field(1), block_field(0)))
        for side in range(2):
            lanes = slice((side + 1) * LANES, (side + 2) * LANES)
            edge_sources[:, lanes] = pieces_of([halo[image, side, comp] for comp in range(COMP)])
        for block in range(2):
            own_flux(block)
        edge = blend(halo_field(1), halo_field(0))
        for comp in range(COMP):
            state[EDGE, comp] = edge[comp]

        if image == 0:
            for block in range(2):
                base_copy(block).wait_recv()
            kept = jnp.where(pack_low, base_far[1], base_far[0])
            other = pltpu.roll(jnp.where(pack_low, base_far[0], base_far[1]), HALO, 1)
            base[EDGE] = jnp.concatenate([kept, other], axis=0).reshape(COMP, NODES, LANES)
            base_gradient(EDGE)

        local_terms(EDGE, pieces_of(edge))
        add_flux(EDGE, edge_sources[...], lambda pair: edge_table[pair])
        for block in range(3):
            state[block] = state[block] + TIME_STEP * acc[block]

        for block in range(2):
            own_terms(block)
        sources[0, :, LANES:SHARD] = pieces_of(blend(block_field(1), block_field(EDGE)))
        sources[1, :, LANES:SHARD] = pieces_of(blend(block_field(EDGE), block_field(0)))
        for block in range(2):
            own_flux(block)
        arrival(image).wait_recv()
        for block in range(2):
            lanes = block_lanes[block]
            value = state[block] + TIME_STEP * acc[block] - follow[image, :, :, lanes]
            (first_ref, second_ref)[image][:, :, lanes] = value
            if image == 0:
                state[block] = value
                halo_copy(1, block).start()
        if image == 0:
            follow_copy(1).start()

    for image in range(2):
        one_image(image)
    for block in range(2):
        for index in range(3):
            list_copy(index, block).wait_send()
        base_copy(block).wait_send()
        for image in range(2):
            halo_copy(image, block).wait_send()
    for image in range(2):
        follow_copy(image).wait_send()


def on_device(base_flow, probe_field, neighbours, face_codes, face_counts):
    operators = operator_pieces()
    field = jax.ShapeDtypeStruct((COMP, NODES, SHARD), jnp.float32)
    vmem = pl.BlockSpec(memory_space=pltpu.VMEM)
    first_image, second_image = pl.pallas_call(
        functools.partial(kernel, lax.axis_size("seg"), lax.axis_size("elem")),
        out_shape=(field, field),
        in_specs=[pl.BlockSpec(memory_space=pltpu.HBM)] * 6,
        out_specs=(vmem, vmem),
        scratch_shapes=[
            pltpu.VMEM(operators.shape, jnp.bfloat16),
            pltpu.VMEM((SLOTS, SHARD), jnp.int32),
            pltpu.VMEM((SLOTS, SHARD), jnp.int32),
            pltpu.VMEM((1, SHARD), jnp.int32),
            pltpu.VMEM((2, SLOTS, LANES), jnp.int32),
            pltpu.VMEM((2, SLOTS, LANES), jnp.int32),
            pltpu.VMEM((2, 1, LANES), jnp.int32),
            pltpu.VMEM((3, COMP, NODES, LANES), jnp.float32),
            pltpu.VMEM((2, 96, LANES), jnp.float32),
            pltpu.VMEM((2, 96, LANES), jnp.float32),
            pltpu.VMEM((3, COMP, NODES, LANES), jnp.float32),
            pltpu.VMEM((3, COMP, NODES, LANES), jnp.float32),
            pltpu.VMEM((3, 3, COMP, NODES, LANES), jnp.float32),
            pltpu.VMEM((3, NODES, LANES), jnp.float32),
            pltpu.VMEM((3, SLOTS, 16, LANES), jnp.int32),
            pltpu.VMEM((3, SLOTS, NODES, LANES), jnp.int32),
            pltpu.VMEM((2, SLOTS // 2, SHARD, SHARD), jnp.bfloat16),
            pltpu.VMEM((SLOTS // 2, 3 * LANES, SHARD), jnp.bfloat16),
            pltpu.VMEM((2, 2 * COMP * NODES, SHARD), jnp.bfloat16),
            pltpu.VMEM((2 * COMP * NODES, 3 * LANES), jnp.bfloat16),
            pltpu.VMEM((2, 2, COMP, NODES, LANES), jnp.float32),
            pltpu.VMEM((2, COMP, NODES, SHARD), jnp.float32),
            pltpu.SemaphoreType.DMA((8,)),
            pltpu.SemaphoreType.DMA((3, 2)),
            pltpu.SemaphoreType.DMA((3, 2)),
            pltpu.SemaphoreType.DMA((2,)),
            pltpu.SemaphoreType.DMA((2,)),
            pltpu.SemaphoreType.DMA((2, 2)),
            pltpu.SemaphoreType.DMA((2, 2)),
            pltpu.SemaphoreType.DMA((2,)),
            pltpu.SemaphoreType.DMA((2,)),
        ],
        compiler_params=pltpu.CompilerParams(
            collective_id=0, has_side_effects=True, vmem_limit_bytes=40 * 1024 * 1024
        ),
        name="shooting",
    )(
        *[
            pltpu.with_memory_space_constraint(value, pltpu.HBM)
            for value in (
                base_flow[0],
                probe_field[0],
                neighbours,
                face_codes,
                face_counts.reshape(1, SHARD),
                operators,
            )
        ]
    )
    return (first_image[None], second_image[None])


def solution(mesh):
    placed = (
        P("seg", None, None, "elem"),
        P("seg", None, None, "elem"),
        P(None, "elem"),
        P(None, "elem"),
        P("elem"),
    )
    return jax.shard_map(
        on_device,
        mesh=mesh,
        in_specs=placed,
        out_specs=(P("seg", None, None, "elem"), P("seg", None, None, "elem")),
        check_vma=False,
    )
```

```python
import functools

import jax
import jax.numpy as jnp
import ml_dtypes
import numpy as np
from jax import lax
from jax.experimental import pallas as pl
from jax.experimental.pallas import tpu as pltpu
from jax.sharding import PartitionSpec as P

STEPS = 2
VISCOSITY = 0.05
PENALTY = 1.0
TIME_STEP = 0.05

COMP = 3
NODES = 64
SHARD = 256
LANES = 128
HALO = 64
EDGE = 2
SLOTS = 6


def operator_tables():
    points = np.array([-1.0, -1.0 / np.sqrt(5.0), 1.0 / np.sqrt(5.0), 1.0])
    barycentric = np.array(
        [
            1.0 / np.prod([points[row] - points[col] for col in range(4) if col != row])
            for row in range(4)
        ]
    )
    derivative = np.zeros((4, 4))
    for row in range(4):
        for col in range(4):
            if row != col:
                derivative[row, col] = (
                    barycentric[col] / barycentric[row] / (points[row] - points[col])
                )
        derivative[row, row] = -np.sum(derivative[row])
    identity = np.eye(4)
    gradient = [
        np.kron(np.kron(derivative, identity), identity),
        np.kron(np.kron(identity, derivative), identity),
        np.kron(np.kron(identity, identity), derivative),
    ]
    laplacian = sum(table @ table for table in gradient)
    return gradient, laplacian


def operator_pieces():
    gradient, laplacian = operator_tables()
    stacked = np.concatenate([VISCOSITY * laplacian] + gradient, axis=0)
    high = stacked.astype(ml_dtypes.bfloat16)
    low = (stacked - high.astype(np.float64)).astype(ml_dtypes.bfloat16)
    return jnp.asarray(np.concatenate([high, high, low, low], axis=1))


def split(value):
    high = value.astype(jnp.bfloat16)
    low = (value - high.astype(jnp.float32)).astype(jnp.bfloat16)
    return high, low


def dot(left, right):
    return jnp.dot(left, right, preferred_element_type=jnp.float32)


def kernel(
    segs,
    elems,
    base_in,
    probe_in,
    near_in,
    code_in,
    count_in,
    oper_in,
    first_ref,
    second_ref,
    oper_ref,
    near_ref,
    code_ref,
    count_ref,
    near_far,
    code_far,
    count_far,
    base,
    base_pack,
    base_far,
    state,
    acc,
    base_grad,
    own_count,
    places,
    targets,
    table,
    edge_table,
    sources,
    edge_sources,
    halo,
    follow,
    ready,
    input_sem,
    list_send,
    list_recv,
    base_send,
    base_recv,
    halo_send,
    halo_recv,
    follow_send,
    follow_recv,
):
    seg = lax.axis_index("seg")
    elem = lax.axis_index("elem")
    right = lax.rem(elem + 1, elems)
    left = lax.rem(elem + elems - 1, elems)
    ahead = lax.rem(seg + 1, segs)
    behind = lax.rem(seg + segs - 1, segs)
    barrier = pltpu.get_barrier_semaphore()
    for target in ({"elem": left}, {"seg": ahead}):
        pl.semaphore_signal(
            barrier, inc=1, device_id=target, device_id_type=pl.DeviceIdType.MESH
        )
    block_lanes = (slice(0, LANES), slice(LANES, SHARD))
    pairs = [(near_in, near_ref), (code_in, code_ref), (count_in, count_ref)]
    for block in range(2):
        pairs.append((probe_in.at[:, :, block_lanes[block]], state.at[block]))
    for block in range(2):
        pairs.append((base_in.at[:, :, block_lanes[block]], base.at[block]))
    pairs.append((oper_in, oper_ref))
    loads = [
        pltpu.make_async_copy(source, target, input_sem.at[index])
        for index, (source, target) in enumerate(pairs)
    ]
    for load in loads:
        load.start()

    def across(source, target, send, recv, block):
        return pltpu.make_async_remote_copy(
            src_ref=source,
            dst_ref=target.at[1 - block],
            send_sem=send.at[block],
            recv_sem=recv.at[1 - block],
            device_id={"elem": (left, right)[block]},
            device_id_type=pl.DeviceIdType.MESH,
        )

    def list_copy(index, block):
        source, target = (
            (near_in, near_far),
            (code_in, code_far),
            (count_in, count_far),
        )[index]
        source = source.at[:, block_lanes[block]]
        return across(source, target, list_send.at[index], list_recv.at[index], block)

    def base_copy(block):
        return across(base_pack.at[block], base_far, base_send, base_recv, block)

    def halo_copy(image, block):
        source = (probe_in, first_ref)[image].at[:, :, block_lanes[block]]
        return across(source, halo.at[image], halo_send.at[image], halo_recv.at[image], block)

    def follow_copy(image):
        return arrival(image, (probe_in, first_ref)[image])

    def arrival(image, source=first_ref):
        return pltpu.make_async_remote_copy(
            src_ref=source,
            dst_ref=follow.at[image],
            send_sem=follow_send.at[image],
            recv_sem=follow_recv.at[image],
            device_id={"seg": behind},
            device_id_type=pl.DeviceIdType.MESH,
        )

    pl.semaphore_wait(barrier, 2)
    pl.semaphore_signal(
        ready, inc=1, device_id={"elem": right}, device_id_type=pl.DeviceIdType.MESH
    )
    for index in range(3):
        list_copy(index, 1).start()
    halo_copy(0, 1).start()
    follow_copy(0).start()

    lane_low = lax.broadcasted_iota(jnp.int32, (NODES, LANES), 1) < HALO
    pack_low = lax.broadcasted_iota(jnp.int32, (96, LANES), 1) < HALO
    list_low = lax.broadcasted_iota(jnp.int32, (SLOTS, LANES), 1) < HALO
    row = lax.broadcasted_iota(jnp.int32, (LANES, LANES), 0)
    slot = lax.broadcasted_iota(jnp.int32, (SLOTS, LANES), 0)
    node = lax.broadcasted_iota(jnp.int32, (NODES, LANES), 0)
    node_at = (
        jnp.right_shift(node, 4),
        jnp.bitwise_and(jnp.right_shift(node, 2), 3),
        jnp.bitwise_and(node, 3),
    )
    trace = lax.broadcasted_iota(jnp.int32, (16, LANES), 0)
    trace_i, trace_j = jnp.right_shift(trace, 2), jnp.bitwise_and(trace, 3)
    blocks = elems * (SHARD // LANES)
    first_block = elem * (SHARD // LANES)

    def one_hot(chosen):
        return jnp.where(row == chosen, 1.0, 0.0).astype(jnp.bfloat16)

    def index_nodes(block, code, live):
        total = jnp.zeros((NODES, LANES), jnp.float32)
        for k in range(SLOTS):
            at = code[k : k + 1]
            way = jnp.right_shift(at, 3)
            end = 3 * jnp.bitwise_and(jnp.right_shift(at, 2), 1)
            turn = jnp.bitwise_and(at, 3)
            far = 3 - end
            place = jnp.where(
                way == 0,
                16 * far + 4 * trace_i + trace_j,
                jnp.where(
                    way == 1,
                    16 * trace_i + 4 * far + trace_j,
                    16 * trace_i + 4 * trace_j + far,
                ),
            )
            places[block, k] = place
            along = jnp.where(way == 0, node_at[0], jnp.where(way == 1, node_at[1], node_at[2]))
            i = jnp.where(way == 0, node_at[1], node_at[0])
            j = jnp.where(way == 2, node_at[1], node_at[2])
            odd = jnp.bitwise_and(turn, 1) == 1
            turned_i, turned_j = jnp.where(odd, j, i), jnp.where(odd, i, j)
            turned_i = jnp.where(turn >= 2, 3 - turned_i, turned_i)
            flip = jnp.logical_or(turn == 1, turn == 2)
            turned_j = jnp.where(flip, 3 - turned_j, turned_j)
            wanted = jnp.where(live[k : k + 1] == 1, end, -1)
            member = along == wanted
            targets[block, k] = jnp.where(member, 4 * turned_i + turned_j, 16)
            total = total + jnp.where(member, 1.0, 0.0)
        own_count[block] = total

    for load in loads[0:3]:
        load.wait()

    def own_lists(block):
        lanes = block_lanes[block]
        near = near_ref[:, lanes]
        used = slot < count_ref[:, lanes]
        place = jnp.where(used, jnp.bitwise_and(near, LANES - 1), -1)
        is_own = jnp.right_shift(near, 7) == first_block + block
        inside, beyond = jnp.where(is_own, place, -1), jnp.where(is_own, -1, place)
        for k in range(SLOTS):
            columns = slice((k % 2) * LANES, (k % 2 + 1) * LANES)
            table[block, k // 2, 0:LANES, columns] = one_hot(inside[k : k + 1])
            table[block, k // 2, LANES:SHARD, columns] = one_hot(beyond[k : k + 1])
        index_nodes(block, code_ref[:, lanes], jnp.where(used, 1, 0))

    def edge_lists():
        near = jnp.where(list_low, near_far[1], near_far[0])
        code = jnp.where(list_low, code_far[1], code_far[0])
        used = slot < jnp.where(list_low[0:1], count_far[1], count_far[0])
        place = jnp.where(used, jnp.bitwise_and(near, LANES - 1), -1)
        outer = jnp.where(
            list_low, lax.rem(first_block + 2, blocks), lax.rem(first_block + blocks - 1, blocks)
        )
        is_outer = jnp.right_shift(near, 7) == outer
        inside, beyond = jnp.where(is_outer, -1, place), jnp.where(is_outer, place, -1)
        to_left, to_right = jnp.where(list_low, -1, beyond), jnp.where(list_low, beyond, -1)
        for k in range(SLOTS):
            columns = slice((k % 2) * LANES, (k % 2 + 1) * LANES)
            for part, chosen in enumerate((inside, to_left, to_right)):
                rows = slice(part * LANES, (part + 1) * LANES)
                edge_table[k // 2, rows, columns] = one_hot(chosen[k : k + 1])
        index_nodes(EDGE, code, jnp.where(used, 1, 0))

    for load in loads[5:7]:
        load.wait()

    def pack_base(block):
        packed = base[block].reshape(COMP * NODES, LANES)
        upper, lower = packed[0:96], pltpu.roll(packed[96:192], HALO, 1)
        base_pack[block] = (
            jnp.where(pack_low, upper, lower) if block == 0 else jnp.where(pack_low, lower, upper)
        )
        base_copy(block).start()

    pack_base(1)
    pl.semaphore_wait(ready, 1)
    for index in range(3):
        list_copy(index, 0).start()
    halo_copy(0, 0).start()
    pack_base(0)
    for block in range(2):
        own_lists(block)

    def pieces_of(fields):
        return jnp.concatenate([piece for field in fields for piece in split(field)], axis=0)

    def derivatives(pieces):
        width = 2 * NODES
        beside = jnp.concatenate(
            [pieces[comp * width : (comp + 1) * width] for comp in range(COMP)], axis=1
        )
        return dot(oper_ref[...], jnp.concatenate([beside, beside], axis=0))

    def base_gradient(block):
        grads = derivatives(pieces_of([base[block, comp] for comp in range(COMP)]))
        for comp in range(COMP):
            lanes = slice(comp * LANES, (comp + 1) * LANES)
            for d in range(3):
                base_grad[block, d, comp] = grads[(d + 1) * NODES : (d + 2) * NODES, lanes]

    loads[7].wait()
    for block in range(2):
        base_gradient(block)
    for load in loads[3:5]:
        load.wait()

    def local_terms(block, pieces):
        grads = derivatives(pieces)
        for comp in range(COMP):
            lanes = slice(comp * LANES, (comp + 1) * LANES)
            total = grads[0:NODES, lanes] - own_count[block] * state[block, comp]
            for d in range(3):
                total = total - base[block, d] * grads[(d + 1) * NODES : (d + 2) * NODES, lanes]
            for d in range(3):
                total = total - state[block, d] * base_grad[block, d, comp]
            acc[block, comp] = total

    def add_flux(block, fields, weights):
        for pair in range(SLOTS // 2):
            found = dot(fields, weights(pair))
            for k in (2 * pair, 2 * pair + 1):
                lanes = slice((k % 2) * LANES, (k % 2 + 1) * LANES)
                place = places[block, k]
                target = targets[block, k]
                lookups = jnp.bitwise_and(place, 7)
                origin = jnp.right_shift(place, 3)
                for comp in range(COMP):
                    at = 2 * comp * NODES
                    value = found[at : at + NODES, lanes]
                    value = value + found[at + NODES : at + 2 * NODES, lanes]
                    halves = []
                    for half, choices in enumerate(((0, 1, 2, 3, 6), (4, 5, 6, 7, 1))):
                        rows = slice(8 * half, 8 * half + 8)
                        picked = None
                        for choice in choices:
                            option = jnp.take_along_axis(
                                value[8 * choice : 8 * choice + 8], lookups[rows], axis=0
                            )
                            picked = (
                                option
                                if picked is None
                                else jnp.where(origin[rows] == choice, option, picked)
                            )
                        halves.append(picked)
                    for group in range(8):
                        rows = slice(8 * group, 8 * group + 8)
                        goal = target[rows]
                        spot = jnp.bitwise_and(goal, 7)
                        turned = jnp.where(
                            goal < 8,
                            jnp.take_along_axis(halves[0], spot, axis=0),
                            jnp.take_along_axis(halves[1], spot, axis=0),
                        )
                        acc[block, comp, rows] += jnp.where(goal < 16, turned, 0.0)

    def blend(low, high):
        return [jnp.where(lane_low, low(comp), high(comp)) for comp in range(COMP)]

    def block_field(block):
        return lambda comp: state[block, comp]

    def own_terms(block):
        pieces = pieces_of([state[block, comp] for comp in range(COMP)])
        sources[block, :, 0:LANES] = pieces
        local_terms(block, pieces)

    def own_flux(block):
        add_flux(block, sources[block], lambda pair: table[block, pair])

    def one_image(image):
        for block in range(2):
            own_terms(block)
        edge_sources[:, 0:LANES] = pieces_of(blend(block_field(0), block_field(1)))

        if image == 0:
            for index in range(3):
                for block in range(2):
                    list_copy(index, block).wait_recv()
            edge_lists()

        for side in range(2):
            across(
                state.at[side], halo.at[image], halo_send.at[image], halo_recv.at[image], 1 - side
            ).wait_recv()

        def halo_field(side):
            return lambda comp: halo[image, side, comp]

        sources[0, :, LANES:SHARD] = pieces_of(blend(block_field(1), halo_field(0)))
        sources[1, :, LANES:SHARD] = pieces_of(blend(halo_field(1), block_field(0)))
        for side in range(2):
            lanes = slice((side + 1) * LANES, (side + 2) * LANES)
            edge_sources[:, lanes] = pieces_of([halo[image, side, comp] for comp in range(COMP)])
        for block in range(2):
            own_flux(block)
        edge = blend(halo_field(1), halo_field(0))
        for comp in range(COMP):
            state[EDGE, comp] = edge[comp]

        if image == 0:
            for block in range(2):
                base_copy(block).wait_recv()
            kept = jnp.where(pack_low, base_far[1], base_far[0])
            other = pltpu.roll(jnp.where(pack_low, base_far[0], base_far[1]), HALO, 1)
            base[EDGE] = jnp.concatenate([kept, other], axis=0).reshape(COMP, NODES, LANES)
            base_gradient(EDGE)

        local_terms(EDGE, pieces_of(edge))
        add_flux(EDGE, edge_sources[...], lambda pair: edge_table[pair])
        for block in range(3):
            state[block] = state[block] + TIME_STEP * acc[block]

        for block in range(2):
            own_terms(block)
        sources[0, :, LANES:SHARD] = pieces_of(blend(block_field(1), block_field(EDGE)))
        sources[1, :, LANES:SHARD] = pieces_of(blend(block_field(EDGE), block_field(0)))
        for block in range(2):
            own_flux(block)
        arrival(image).wait_recv()
        for block in range(2):
            lanes = block_lanes[block]
            value = state[block] + TIME_STEP * acc[block] - follow[image, :, :, lanes]
            (first_ref, second_ref)[image][:, :, lanes] = value
            if image == 0:
                state[block] = value
                halo_copy(1, block).start()
        if image == 0:
            follow_copy(1).start()

    for image in range(2):
        one_image(image)
    for block in range(2):
        for index in range(3):
            list_copy(index, block).wait_send()
        base_copy(block).wait_send()
        for image in range(2):
            halo_copy(image, block).wait_send()
    for image in range(2):
        follow_copy(image).wait_send()


def on_device(base_flow, probe_field, neighbours, face_codes, face_counts):
    operators = operator_pieces()
    field = jax.ShapeDtypeStruct((COMP, NODES, SHARD), jnp.float32)
    vmem = pl.BlockSpec(memory_space=pltpu.VMEM)
    first_image, second_image = pl.pallas_call(
        functools.partial(kernel, lax.axis_size("seg"), lax.axis_size("elem")),
        out_shape=(field, field),
        in_specs=[pl.BlockSpec(memory_space=pltpu.HBM)] * 6,
        out_specs=(vmem, vmem),
        scratch_shapes=[
            pltpu.VMEM(operators.shape, jnp.bfloat16),
            pltpu.VMEM((SLOTS, SHARD), jnp.int32),
            pltpu.VMEM((SLOTS, SHARD), jnp.int32),
            pltpu.VMEM((1, SHARD), jnp.int32),
            pltpu.VMEM((2, SLOTS, LANES), jnp.int32),
            pltpu.VMEM((2, SLOTS, LANES), jnp.int32),
            pltpu.VMEM((2, 1, LANES), jnp.int32),
            pltpu.VMEM((3, COMP, NODES, LANES), jnp.float32),
            pltpu.VMEM((2, 96, LANES), jnp.float32),
            pltpu.VMEM((2, 96, LANES), jnp.float32),
            pltpu.VMEM((3, COMP, NODES, LANES), jnp.float32),
            pltpu.VMEM((3, COMP, NODES, LANES), jnp.float32),
            pltpu.VMEM((3, 3, COMP, NODES, LANES), jnp.float32),
            pltpu.VMEM((3, NODES, LANES), jnp.float32),
            pltpu.VMEM((3, SLOTS, 16, LANES), jnp.int32),
            pltpu.VMEM((3, SLOTS, NODES, LANES), jnp.int32),
            pltpu.VMEM((2, SLOTS // 2, SHARD, SHARD), jnp.bfloat16),
            pltpu.VMEM((SLOTS // 2, 3 * LANES, SHARD), jnp.bfloat16),
            pltpu.VMEM((2, 2 * COMP * NODES, SHARD), jnp.bfloat16),
            pltpu.VMEM((2 * COMP * NODES, 3 * LANES), jnp.bfloat16),
            pltpu.VMEM((2, 2, COMP, NODES, LANES), jnp.float32),
            pltpu.VMEM((2, COMP, NODES, SHARD), jnp.float32),
            pltpu.SemaphoreType.REGULAR,
            pltpu.SemaphoreType.DMA((8,)),
            pltpu.SemaphoreType.DMA((3, 2)),
            pltpu.SemaphoreType.DMA((3, 2)),
            pltpu.SemaphoreType.DMA((2,)),
            pltpu.SemaphoreType.DMA((2,)),
            pltpu.SemaphoreType.DMA((2, 2)),
            pltpu.SemaphoreType.DMA((2, 2)),
            pltpu.SemaphoreType.DMA((2,)),
            pltpu.SemaphoreType.DMA((2,)),
        ],
        compiler_params=pltpu.CompilerParams(
            collective_id=0, has_side_effects=True, vmem_limit_bytes=40 * 1024 * 1024
        ),
        name="shooting",
    )(
        *[
            pltpu.with_memory_space_constraint(value, pltpu.HBM)
            for value in (
                base_flow[0],
                probe_field[0],
                neighbours,
                face_codes,
                face_counts.reshape(1, SHARD),
                operators,
            )
        ]
    )
    return (first_image[None], second_image[None])


def solution(mesh):
    placed = (
        P("seg", None, None, "elem"),
        P("seg", None, None, "elem"),
        P(None, "elem"),
        P(None, "elem"),
        P("elem"),
    )
    return jax.shard_map(
        on_device,
        mesh=mesh,
        in_specs=placed,
        out_specs=(P("seg", None, None, "elem"), P("seg", None, None, "elem")),
        check_vma=False,
    )
```

```python
import functools

import jax
import jax.numpy as jnp
import ml_dtypes
import numpy as np
from jax import lax
from jax.experimental import pallas as pl
from jax.experimental.pallas import tpu as pltpu
from jax.sharding import PartitionSpec as P

STEPS = 2
VISCOSITY = 0.05
PENALTY = 1.0
TIME_STEP = 0.05

COMP = 3
NODES = 64
SHARD = 256
LANES = 128
HALO = 64
EDGE = 2
SLOTS = 6


def operator_tables():
    points = np.array([-1.0, -1.0 / np.sqrt(5.0), 1.0 / np.sqrt(5.0), 1.0])
    barycentric = np.array(
        [
            1.0 / np.prod([points[row] - points[col] for col in range(4) if col != row])
            for row in range(4)
        ]
    )
    derivative = np.zeros((4, 4))
    for row in range(4):
        for col in range(4):
            if row != col:
                derivative[row, col] = (
                    barycentric[col] / barycentric[row] / (points[row] - points[col])
                )
        derivative[row, row] = -np.sum(derivative[row])
    identity = np.eye(4)
    gradient = [
        np.kron(np.kron(derivative, identity), identity),
        np.kron(np.kron(identity, derivative), identity),
        np.kron(np.kron(identity, identity), derivative),
    ]
    laplacian = sum(table @ table for table in gradient)
    return gradient, laplacian


def operator_pieces():
    gradient, laplacian = operator_tables()
    stacked = np.concatenate([VISCOSITY * laplacian] + gradient, axis=0)
    high = stacked.astype(ml_dtypes.bfloat16)
    low = (stacked - high.astype(np.float64)).astype(ml_dtypes.bfloat16)
    return jnp.asarray(np.concatenate([high, high, low, low], axis=1))


def split(value):
    high = value.astype(jnp.bfloat16)
    low = (value - high.astype(jnp.float32)).astype(jnp.bfloat16)
    return high, low


def dot(left, right):
    return jnp.dot(left, right, preferred_element_type=jnp.float32)


def kernel(
    segs,
    elems,
    base_in,
    probe_in,
    near_in,
    code_in,
    count_in,
    oper_in,
    first_ref,
    second_ref,
    oper_ref,
    near_ref,
    code_ref,
    count_ref,
    near_far,
    code_far,
    count_far,
    base,
    base_pack,
    base_far,
    state,
    acc,
    base_grad,
    own_count,
    places,
    targets,
    table,
    edge_table,
    sources,
    edge_sources,
    halo,
    follow,
    ready,
    input_sem,
    list_send,
    list_recv,
    base_send,
    base_recv,
    halo_send,
    halo_recv,
    follow_send,
    follow_recv,
):
    seg = lax.axis_index("seg")
    elem = lax.axis_index("elem")
    right = lax.rem(elem + 1, elems)
    left = lax.rem(elem + elems - 1, elems)
    ahead = lax.rem(seg + 1, segs)
    behind = lax.rem(seg + segs - 1, segs)
    barrier = pltpu.get_barrier_semaphore()
    for target in ({"elem": left}, {"seg": ahead}):
        pl.semaphore_signal(
            barrier, inc=1, device_id=target, device_id_type=pl.DeviceIdType.MESH
        )
    block_lanes = (slice(0, LANES), slice(LANES, SHARD))
    pairs = [(near_in, near_ref), (code_in, code_ref), (count_in, count_ref)]
    for block in range(2):
        pairs.append((probe_in.at[:, :, block_lanes[block]], state.at[block]))
    for block in range(2):
        pairs.append((base_in.at[:, :, block_lanes[block]], base.at[block]))
    pairs.append((oper_in, oper_ref))
    loads = [
        pltpu.make_async_copy(source, target, input_sem.at[index])
        for index, (source, target) in enumerate(pairs)
    ]
    for load in loads:
        load.start()

    def across(source, target, send, recv, block):
        return pltpu.make_async_remote_copy(
            src_ref=source,
            dst_ref=target.at[1 - block],
            send_sem=send.at[block],
            recv_sem=recv.at[1 - block],
            device_id={"elem": (left, right)[block]},
            device_id_type=pl.DeviceIdType.MESH,
        )

    def list_copy(index, block):
        source, target = (
            (near_in, near_far),
            (code_in, code_far),
            (count_in, count_far),
        )[index]
        source = source.at[:, block_lanes[block]]
        return across(source, target, list_send.at[index], list_recv.at[index], block)

    def base_copy(block):
        return across(base_pack.at[block], base_far, base_send, base_recv, block)

    def halo_copy(image, block):
        source = (probe_in, first_ref)[image].at[:, :, block_lanes[block]]
        return across(source, halo.at[image], halo_send.at[image], halo_recv.at[image], block)

    def follow_copy(image):
        return arrival(image, (probe_in, first_ref)[image])

    def arrival(image, source=first_ref):
        return pltpu.make_async_remote_copy(
            src_ref=source,
            dst_ref=follow.at[image],
            send_sem=follow_send.at[image],
            recv_sem=follow_recv.at[image],
            device_id={"seg": behind},
            device_id_type=pl.DeviceIdType.MESH,
        )

    pl.semaphore_wait(barrier, 2)
    pl.semaphore_signal(
        ready, inc=1, device_id={"elem": right}, device_id_type=pl.DeviceIdType.MESH
    )
    for index in range(3):
        list_copy(index, 1).start()
    halo_copy(0, 1).start()

    lane_low = lax.broadcasted_iota(jnp.int32, (NODES, LANES), 1) < HALO
    pack_low = lax.broadcasted_iota(jnp.int32, (96, LANES), 1) < HALO
    list_low = lax.broadcasted_iota(jnp.int32, (SLOTS, LANES), 1) < HALO
    row = lax.broadcasted_iota(jnp.int32, (LANES, LANES), 0)
    slot = lax.broadcasted_iota(jnp.int32, (SLOTS, LANES), 0)
    node = lax.broadcasted_iota(jnp.int32, (NODES, LANES), 0)
    node_at = (
        jnp.right_shift(node, 4),
        jnp.bitwise_and(jnp.right_shift(node, 2), 3),
        jnp.bitwise_and(node, 3),
    )
    trace = lax.broadcasted_iota(jnp.int32, (16, LANES), 0)
    trace_i, trace_j = jnp.right_shift(trace, 2), jnp.bitwise_and(trace, 3)
    blocks = elems * (SHARD // LANES)
    first_block = elem * (SHARD // LANES)

    def one_hot(chosen):
        return jnp.where(row == chosen, 1.0, 0.0).astype(jnp.bfloat16)

    def index_nodes(block, code, live):
        total = jnp.zeros((NODES, LANES), jnp.float32)
        for k in range(SLOTS):
            at = code[k : k + 1]
            way = jnp.right_shift(at, 3)
            end = 3 * jnp.bitwise_and(jnp.right_shift(at, 2), 1)
            turn = jnp.bitwise_and(at, 3)
            far = 3 - end
            place = jnp.where(
                way == 0,
                16 * far + 4 * trace_i + trace_j,
                jnp.where(
                    way == 1,
                    16 * trace_i + 4 * far + trace_j,
                    16 * trace_i + 4 * trace_j + far,
                ),
            )
            places[block, k] = place
            along = jnp.where(way == 0, node_at[0], jnp.where(way == 1, node_at[1], node_at[2]))
            i = jnp.where(way == 0, node_at[1], node_at[0])
            j = jnp.where(way == 2, node_at[1], node_at[2])
            odd = jnp.bitwise_and(turn, 1) == 1
            turned_i, turned_j = jnp.where(odd, j, i), jnp.where(odd, i, j)
            turned_i = jnp.where(turn >= 2, 3 - turned_i, turned_i)
            flip = jnp.logical_or(turn == 1, turn == 2)
            turned_j = jnp.where(flip, 3 - turned_j, turned_j)
            wanted = jnp.where(live[k : k + 1] == 1, end, -1)
            member = along == wanted
            targets[block, k] = jnp.where(member, 4 * turned_i + turned_j, 16)
            total = total + jnp.where(member, 1.0, 0.0)
        own_count[block] = total

    for load in loads[0:3]:
        load.wait()

    def own_lists(block):
        lanes = block_lanes[block]
        near = near_ref[:, lanes]
        used = slot < count_ref[:, lanes]
        place = jnp.where(used, jnp.bitwise_and(near, LANES - 1), -1)
        is_own = jnp.right_shift(near, 7) == first_block + block
        inside, beyond = jnp.where(is_own, place, -1), jnp.where(is_own, -1, place)
        for k in range(SLOTS):
            columns = slice((k % 2) * LANES, (k % 2 + 1) * LANES)
            table[block, k // 2, 0:LANES, columns] = one_hot(inside[k : k + 1])
            table[block, k // 2, LANES:SHARD, columns] = one_hot(beyond[k : k + 1])
        index_nodes(block, code_ref[:, lanes], jnp.where(used, 1, 0))

    def edge_lists():
        near = jnp.where(list_low, near_far[1], near_far[0])
        code = jnp.where(list_low, code_far[1], code_far[0])
        used = slot < jnp.where(list_low[0:1], count_far[1], count_far[0])
        place = jnp.where(used, jnp.bitwise_and(near, LANES - 1), -1)
        outer = jnp.where(
            list_low, lax.rem(first_block + 2, blocks), lax.rem(first_block + blocks - 1, blocks)
        )
        is_outer = jnp.right_shift(near, 7) == outer
        inside, beyond = jnp.where(is_outer, -1, place), jnp.where(is_outer, place, -1)
        to_left, to_right = jnp.where(list_low, -1, beyond), jnp.where(list_low, beyond, -1)
        for k in range(SLOTS):
            columns = slice((k % 2) * LANES, (k % 2 + 1) * LANES)
            for part, chosen in enumerate((inside, to_left, to_right)):
                rows = slice(part * LANES, (part + 1) * LANES)
                edge_table[k // 2, rows, columns] = one_hot(chosen[k : k + 1])
        index_nodes(EDGE, code, jnp.where(used, 1, 0))

    for load in loads[5:7]:
        load.wait()

    def pack_base(block):
        packed = base[block].reshape(COMP * NODES, LANES)
        upper, lower = packed[0:96], pltpu.roll(packed[96:192], HALO, 1)
        base_pack[block] = (
            jnp.where(pack_low, upper, lower) if block == 0 else jnp.where(pack_low, lower, upper)
        )
        base_copy(block).start()

    pack_base(1)
    follow_copy(0).start()
    pl.semaphore_wait(ready, 1)
    for index in range(3):
        list_copy(index, 0).start()
    halo_copy(0, 0).start()
    pack_base(0)
    for block in range(2):
        own_lists(block)

    def pieces_of(fields):
        return jnp.concatenate([piece for field in fields for piece in split(field)], axis=0)

    def derivatives(pieces):
        width = 2 * NODES
        beside = jnp.concatenate(
            [pieces[comp * width : (comp + 1) * width] for comp in range(COMP)], axis=1
        )
        return dot(oper_ref[...], jnp.concatenate([beside, beside], axis=0))

    def base_gradient(block):
        grads = derivatives(pieces_of([base[block, comp] for comp in range(COMP)]))
        for comp in range(COMP):
            lanes = slice(comp * LANES, (comp + 1) * LANES)
            for d in range(3):
                base_grad[block, d, comp] = grads[(d + 1) * NODES : (d + 2) * NODES, lanes]

    loads[7].wait()
    for block in range(2):
        base_gradient(block)
    for load in loads[3:5]:
        load.wait()

    def local_terms(block, pieces):
        grads = derivatives(pieces)
        for comp in range(COMP):
            lanes = slice(comp * LANES, (comp + 1) * LANES)
            total = grads[0:NODES, lanes] - own_count[block] * state[block, comp]
            for d in range(3):
                total = total - base[block, d] * grads[(d + 1) * NODES : (d + 2) * NODES, lanes]
            for d in range(3):
                total = total - state[block, d] * base_grad[block, d, comp]
            acc[block, comp] = total

    def add_flux(block, fields, weights):
        for pair in range(SLOTS // 2):
            found = dot(fields, weights(pair))
            for k in (2 * pair, 2 * pair + 1):
                lanes = slice((k % 2) * LANES, (k % 2 + 1) * LANES)
                place = places[block, k]
                target = targets[block, k]
                lookups = jnp.bitwise_and(place, 7)
                origin = jnp.right_shift(place, 3)
                for comp in range(COMP):
                    at = 2 * comp * NODES
                    value = found[at : at + NODES, lanes]
                    value = value + found[at + NODES : at + 2 * NODES, lanes]
                    halves = []
                    for half, choices in enumerate(((0, 1, 2, 3, 6), (4, 5, 6, 7, 1))):
                        rows = slice(8 * half, 8 * half + 8)
                        picked = None
                        for choice in choices:
                            option = jnp.take_along_axis(
                                value[8 * choice : 8 * choice + 8], lookups[rows], axis=0
                            )
                            picked = (
                                option
                                if picked is None
                                else jnp.where(origin[rows] == choice, option, picked)
                            )
                        halves.append(picked)
                    for group in range(8):
                        rows = slice(8 * group, 8 * group + 8)
                        goal = target[rows]
                        spot = jnp.bitwise_and(goal, 7)
                        turned = jnp.where(
                            goal < 8,
                            jnp.take_along_axis(halves[0], spot, axis=0),
                            jnp.take_along_axis(halves[1], spot, axis=0),
                        )
                        acc[block, comp, rows] += jnp.where(goal < 16, turned, 0.0)

    def blend(low, high):
        return [jnp.where(lane_low, low(comp), high(comp)) for comp in range(COMP)]

    def block_field(block):
        return lambda comp: state[block, comp]

    def own_terms(block):
        pieces = pieces_of([state[block, comp] for comp in range(COMP)])
        sources[block, :, 0:LANES] = pieces
        local_terms(block, pieces)

    def own_flux(block):
        add_flux(block, sources[block], lambda pair: table[block, pair])

    def one_image(image):
        for block in range(2):
            own_terms(block)
        edge_sources[:, 0:LANES] = pieces_of(blend(block_field(0), block_field(1)))

        if image == 0:
            for index in range(3):
                for block in range(2):
                    list_copy(index, block).wait_recv()
            edge_lists()

        for side in range(2):
            across(
                state.at[side], halo.at[image], halo_send.at[image], halo_recv.at[image], 1 - side
            ).wait_recv()

        def halo_field(side):
            return lambda comp: halo[image, side, comp]

        sources[0, :, LANES:SHARD] = pieces_of(blend(block_field(1), halo_field(0)))
        sources[1, :, LANES:SHARD] = pieces_of(blend(halo_field(1), block_field(0)))
        for side in range(2):
            lanes = slice((side + 1) * LANES, (side + 2) * LANES)
            edge_sources[:, lanes] = pieces_of([halo[image, side, comp] for comp in range(COMP)])
        for block in range(2):
            own_flux(block)
        edge = blend(halo_field(1), halo_field(0))
        for comp in range(COMP):
            state[EDGE, comp] = edge[comp]

        if image == 0:
            for block in range(2):
                base_copy(block).wait_recv()
            kept = jnp.where(pack_low, base_far[1], base_far[0])
            other = pltpu.roll(jnp.where(pack_low, base_far[0], base_far[1]), HALO, 1)
            base[EDGE] = jnp.concatenate([kept, other], axis=0).reshape(COMP, NODES, LANES)
            base_gradient(EDGE)

        local_terms(EDGE, pieces_of(edge))
        add_flux(EDGE, edge_sources[...], lambda pair: edge_table[pair])
        for block in range(3):
            state[block] = state[block] + TIME_STEP * acc[block]

        for block in range(2):
            own_terms(block)
        sources[0, :, LANES:SHARD] = pieces_of(blend(block_field(1), block_field(EDGE)))
        sources[1, :, LANES:SHARD] = pieces_of(blend(block_field(EDGE), block_field(0)))
        for block in range(2):
            own_flux(block)
        arrival(image).wait_recv()
        for block in range(2):
            lanes = block_lanes[block]
            value = state[block] + TIME_STEP * acc[block] - follow[image, :, :, lanes]
            (first_ref, second_ref)[image][:, :, lanes] = value
            if image == 0:
                state[block] = value
                halo_copy(1, block).start()
        if image == 0:
            follow_copy(1).start()

    for image in range(2):
        one_image(image)
    for block in range(2):
        for index in range(3):
            list_copy(index, block).wait_send()
        base_copy(block).wait_send()
        for image in range(2):
            halo_copy(image, block).wait_send()
    for image in range(2):
        follow_copy(image).wait_send()


def on_device(base_flow, probe_field, neighbours, face_codes, face_counts):
    operators = operator_pieces()
    field = jax.ShapeDtypeStruct((COMP, NODES, SHARD), jnp.float32)
    vmem = pl.BlockSpec(memory_space=pltpu.VMEM)
    first_image, second_image = pl.pallas_call(
        functools.partial(kernel, lax.axis_size("seg"), lax.axis_size("elem")),
        out_shape=(field, field),
        in_specs=[pl.BlockSpec(memory_space=pltpu.HBM)] * 6,
        out_specs=(vmem, vmem),
        scratch_shapes=[
            pltpu.VMEM(operators.shape, jnp.bfloat16),
            pltpu.VMEM((SLOTS, SHARD), jnp.int32),
            pltpu.VMEM((SLOTS, SHARD), jnp.int32),
            pltpu.VMEM((1, SHARD), jnp.int32),
            pltpu.VMEM((2, SLOTS, LANES), jnp.int32),
            pltpu.VMEM((2, SLOTS, LANES), jnp.int32),
            pltpu.VMEM((2, 1, LANES), jnp.int32),
            pltpu.VMEM((3, COMP, NODES, LANES), jnp.float32),
            pltpu.VMEM((2, 96, LANES), jnp.float32),
            pltpu.VMEM((2, 96, LANES), jnp.float32),
            pltpu.VMEM((3, COMP, NODES, LANES), jnp.float32),
            pltpu.VMEM((3, COMP, NODES, LANES), jnp.float32),
            pltpu.VMEM((3, 3, COMP, NODES, LANES), jnp.float32),
            pltpu.VMEM((3, NODES, LANES), jnp.float32),
            pltpu.VMEM((3, SLOTS, 16, LANES), jnp.int32),
            pltpu.VMEM((3, SLOTS, NODES, LANES), jnp.int32),
            pltpu.VMEM((2, SLOTS // 2, SHARD, SHARD), jnp.bfloat16),
            pltpu.VMEM((SLOTS // 2, 3 * LANES, SHARD), jnp.bfloat16),
            pltpu.VMEM((2, 2 * COMP * NODES, SHARD), jnp.bfloat16),
            pltpu.VMEM((2 * COMP * NODES, 3 * LANES), jnp.bfloat16),
            pltpu.VMEM((2, 2, COMP, NODES, LANES), jnp.float32),
            pltpu.VMEM((2, COMP, NODES, SHARD), jnp.float32),
            pltpu.SemaphoreType.REGULAR,
            pltpu.SemaphoreType.DMA((8,)),
            pltpu.SemaphoreType.DMA((3, 2)),
            pltpu.SemaphoreType.DMA((3, 2)),
            pltpu.SemaphoreType.DMA((2,)),
            pltpu.SemaphoreType.DMA((2,)),
            pltpu.SemaphoreType.DMA((2, 2)),
            pltpu.SemaphoreType.DMA((2, 2)),
            pltpu.SemaphoreType.DMA((2,)),
            pltpu.SemaphoreType.DMA((2,)),
        ],
        compiler_params=pltpu.CompilerParams(
            collective_id=0, has_side_effects=True, vmem_limit_bytes=40 * 1024 * 1024
        ),
        name="shooting",
    )(
        *[
            pltpu.with_memory_space_constraint(value, pltpu.HBM)
            for value in (
                base_flow[0],
                probe_field[0],
                neighbours,
                face_codes,
                face_counts.reshape(1, SHARD),
                operators,
            )
        ]
    )
    return (first_image[None], second_image[None])


def solution(mesh):
    placed = (
        P("seg", None, None, "elem"),
        P("seg", None, None, "elem"),
        P(None, "elem"),
        P(None, "elem"),
        P("elem"),
    )
    return jax.shard_map(
        on_device,
        mesh=mesh,
        in_specs=placed,
        out_specs=(P("seg", None, None, "elem"), P("seg", None, None, "elem")),
        check_vma=False,
    )
```

```python
import functools

import jax
import jax.numpy as jnp
import ml_dtypes
import numpy as np
from jax import lax
from jax.experimental import pallas as pl
from jax.experimental.pallas import tpu as pltpu
from jax.sharding import PartitionSpec as P

STEPS = 2
VISCOSITY = 0.05
PENALTY = 1.0
TIME_STEP = 0.05

COMP = 3
NODES = 64
SHARD = 256
LANES = 128
HALO = 64
EDGE = 2
SLOTS = 6


def operator_tables():
    points = np.array([-1.0, -1.0 / np.sqrt(5.0), 1.0 / np.sqrt(5.0), 1.0])
    barycentric = np.array(
        [
            1.0 / np.prod([points[row] - points[col] for col in range(4) if col != row])
            for row in range(4)
        ]
    )
    derivative = np.zeros((4, 4))
    for row in range(4):
        for col in range(4):
            if row != col:
                derivative[row, col] = (
                    barycentric[col] / barycentric[row] / (points[row] - points[col])
                )
        derivative[row, row] = -np.sum(derivative[row])
    identity = np.eye(4)
    gradient = [
        np.kron(np.kron(derivative, identity), identity),
        np.kron(np.kron(identity, derivative), identity),
        np.kron(np.kron(identity, identity), derivative),
    ]
    laplacian = sum(table @ table for table in gradient)
    return gradient, laplacian


def operator_pieces():
    gradient, laplacian = operator_tables()
    stacked = np.concatenate([VISCOSITY * laplacian] + gradient, axis=0)
    high = stacked.astype(ml_dtypes.bfloat16)
    low = (stacked - high.astype(np.float64)).astype(ml_dtypes.bfloat16)
    return jnp.asarray(np.concatenate([high, high, low, low], axis=1))


def split(value):
    high = value.astype(jnp.bfloat16)
    low = (value - high.astype(jnp.float32)).astype(jnp.bfloat16)
    return high, low


def dot(left, right):
    return jnp.dot(left, right, preferred_element_type=jnp.float32)


def kernel(
    segs,
    elems,
    base_in,
    probe_in,
    near_in,
    code_in,
    count_in,
    oper_in,
    first_ref,
    second_ref,
    oper_ref,
    near_ref,
    code_ref,
    count_ref,
    near_far,
    code_far,
    count_far,
    base,
    base_pack,
    base_far,
    state,
    acc,
    base_grad,
    own_count,
    places,
    targets,
    table,
    edge_table,
    sources,
    edge_sources,
    halo,
    follow,
    input_sem,
    list_send,
    list_recv,
    base_send,
    base_recv,
    halo_send,
    halo_recv,
    follow_send,
    follow_recv,
):
    seg = lax.axis_index("seg")
    elem = lax.axis_index("elem")
    right = lax.rem(elem + 1, elems)
    left = lax.rem(elem + elems - 1, elems)
    ahead = lax.rem(seg + 1, segs)
    behind = lax.rem(seg + segs - 1, segs)
    barrier = pltpu.get_barrier_semaphore()
    for target in ({"elem": left}, {"elem": right}, {"seg": ahead}):
        pl.semaphore_signal(
            barrier, inc=1, device_id=target, device_id_type=pl.DeviceIdType.MESH
        )
    block_lanes = (slice(0, LANES), slice(LANES, SHARD))
    pairs = [(near_in, near_ref), (code_in, code_ref), (count_in, count_ref)]
    for block in range(2):
        pairs.append((probe_in.at[:, :, block_lanes[block]], state.at[block]))
    for block in range(2):
        pairs.append((base_in.at[:, :, block_lanes[block]], base.at[block]))
    pairs.append((oper_in, oper_ref))
    loads = [
        pltpu.make_async_copy(source, target, input_sem.at[index])
        for index, (source, target) in enumerate(pairs)
    ]
    for load in loads:
        load.start()

    def across(source, target, send, recv, block):
        return pltpu.make_async_remote_copy(
            src_ref=source,
            dst_ref=target.at[1 - block],
            send_sem=send.at[block],
            recv_sem=recv.at[1 - block],
            device_id={"elem": (left, right)[block]},
            device_id_type=pl.DeviceIdType.MESH,
        )

    def list_copy(index, block):
        source, target = (
            (near_in, near_far),
            (code_in, code_far),
            (count_in, count_far),
        )[index]
        source = source.at[:, block_lanes[block]]
        return across(source, target, list_send.at[index], list_recv.at[index], block)

    def base_copy(block):
        return across(base_pack.at[block], base_far, base_send, base_recv, block)

    def halo_copy(image, block):
        source = (probe_in, first_ref)[image].at[:, :, block_lanes[block]]
        return across(source, halo.at[image], halo_send.at[image], halo_recv.at[image], block)

    def follow_copy(image, block):
        return arrival(image, block, (probe_in, first_ref)[image])

    def arrival(image, block, source=first_ref):
        lanes = block_lanes[block]
        return pltpu.make_async_remote_copy(
            src_ref=source.at[:, :, lanes],
            dst_ref=follow.at[image, :, :, lanes],
            send_sem=follow_send.at[image, block],
            recv_sem=follow_recv.at[image, block],
            device_id={"seg": behind},
            device_id_type=pl.DeviceIdType.MESH,
        )

    pl.semaphore_wait(barrier, 3)
    for index in range(3):
        for block in range(2):
            list_copy(index, block).start()
    for block in range(2):
        halo_copy(0, block).start()

    lane_low = lax.broadcasted_iota(jnp.int32, (NODES, LANES), 1) < HALO
    pack_low = lax.broadcasted_iota(jnp.int32, (96, LANES), 1) < HALO
    list_low = lax.broadcasted_iota(jnp.int32, (SLOTS, LANES), 1) < HALO
    row = lax.broadcasted_iota(jnp.int32, (LANES, LANES), 0)
    slot = lax.broadcasted_iota(jnp.int32, (SLOTS, LANES), 0)
    node = lax.broadcasted_iota(jnp.int32, (NODES, LANES), 0)
    node_at = (
        jnp.right_shift(node, 4),
        jnp.bitwise_and(jnp.right_shift(node, 2), 3),
        jnp.bitwise_and(node, 3),
    )
    trace = lax.broadcasted_iota(jnp.int32, (16, LANES), 0)
    trace_i, trace_j = jnp.right_shift(trace, 2), jnp.bitwise_and(trace, 3)
    blocks = elems * (SHARD // LANES)
    first_block = elem * (SHARD // LANES)

    def one_hot(chosen):
        return jnp.where(row == chosen, 1.0, 0.0).astype(jnp.bfloat16)

    def index_nodes(block, code, live):
        total = jnp.zeros((NODES, LANES), jnp.float32)
        for k in range(SLOTS):
            at = code[k : k + 1]
            way = jnp.right_shift(at, 3)
            end = 3 * jnp.bitwise_and(jnp.right_shift(at, 2), 1)
            turn = jnp.bitwise_and(at, 3)
            far = 3 - end
            place = jnp.where(
                way == 0,
                16 * far + 4 * trace_i + trace_j,
                jnp.where(
                    way == 1,
                    16 * trace_i + 4 * far + trace_j,
                    16 * trace_i + 4 * trace_j + far,
                ),
            )
            places[block, k] = place
            along = jnp.where(way == 0, node_at[0], jnp.where(way == 1, node_at[1], node_at[2]))
            i = jnp.where(way == 0, node_at[1], node_at[0])
            j = jnp.where(way == 2, node_at[1], node_at[2])
            odd = jnp.bitwise_and(turn, 1) == 1
            turned_i, turned_j = jnp.where(odd, j, i), jnp.where(odd, i, j)
            turned_i = jnp.where(turn >= 2, 3 - turned_i, turned_i)
            flip = jnp.logical_or(turn == 1, turn == 2)
            turned_j = jnp.where(flip, 3 - turned_j, turned_j)
            wanted = jnp.where(live[k : k + 1] == 1, end, -1)
            member = along == wanted
            targets[block, k] = jnp.where(member, 4 * turned_i + turned_j, 16)
            total = total + jnp.where(member, 1.0, 0.0)
        own_count[block] = total

    for load in loads[0:3]:
        load.wait()

    def own_lists(block):
        lanes = block_lanes[block]
        near = near_ref[:, lanes]
        used = slot < count_ref[:, lanes]
        place = jnp.where(used, jnp.bitwise_and(near, LANES - 1), -1)
        is_own = jnp.right_shift(near, 7) == first_block + block
        inside, beyond = jnp.where(is_own, place, -1), jnp.where(is_own, -1, place)
        for k in range(SLOTS):
            columns = slice((k % 2) * LANES, (k % 2 + 1) * LANES)
            table[block, k // 2, 0:LANES, columns] = one_hot(inside[k : k + 1])
            table[block, k // 2, LANES:SHARD, columns] = one_hot(beyond[k : k + 1])
        index_nodes(block, code_ref[:, lanes], jnp.where(used, 1, 0))

    def edge_lists():
        near = jnp.where(list_low, near_far[1], near_far[0])
        code = jnp.where(list_low, code_far[1], code_far[0])
        used = slot < jnp.where(list_low[0:1], count_far[1], count_far[0])
        place = jnp.where(used, jnp.bitwise_and(near, LANES - 1), -1)
        outer = jnp.where(
            list_low, lax.rem(first_block + 2, blocks), lax.rem(first_block + blocks - 1, blocks)
        )
        is_outer = jnp.right_shift(near, 7) == outer
        inside, beyond = jnp.where(is_outer, -1, place), jnp.where(is_outer, place, -1)
        to_left, to_right = jnp.where(list_low, -1, beyond), jnp.where(list_low, beyond, -1)
        for k in range(SLOTS):
            columns = slice((k % 2) * LANES, (k % 2 + 1) * LANES)
            for part, chosen in enumerate((inside, to_left, to_right)):
                rows = slice(part * LANES, (part + 1) * LANES)
                edge_table[k // 2, rows, columns] = one_hot(chosen[k : k + 1])
        index_nodes(EDGE, code, jnp.where(used, 1, 0))

    for load in loads[5:7]:
        load.wait()
    for block in range(2):
        packed = base[block].reshape(COMP * NODES, LANES)
        upper, lower = packed[0:96], pltpu.roll(packed[96:192], HALO, 1)
        base_pack[block] = (
            jnp.where(pack_low, upper, lower) if block == 0 else jnp.where(pack_low, lower, upper)
        )
        base_copy(block).start()
    for block in (1, 0):
        follow_copy(0, block).start()
    for block in range(2):
        own_lists(block)

    def pieces_of(fields):
        return jnp.concatenate([piece for field in fields for piece in split(field)], axis=0)

    def derivatives(pieces):
        width = 2 * NODES
        beside = jnp.concatenate(
            [pieces[comp * width : (comp + 1) * width] for comp in range(COMP)], axis=1
        )
        return dot(oper_ref[...], jnp.concatenate([beside, beside], axis=0))

    def base_gradient(block):
        grads = derivatives(pieces_of([base[block, comp] for comp in range(COMP)]))
        for comp in range(COMP):
            lanes = slice(comp * LANES, (comp + 1) * LANES)
            for d in range(3):
                base_grad[block, d, comp] = grads[(d + 1) * NODES : (d + 2) * NODES, lanes]

    loads[7].wait()
    for block in range(2):
        base_gradient(block)
    for load in loads[3:5]:
        load.wait()

    def local_terms(block, pieces):
        grads = derivatives(pieces)
        for comp in range(COMP):
            lanes = slice(comp * LANES, (comp + 1) * LANES)
            total = grads[0:NODES, lanes] - own_count[block] * state[block, comp]
            for d in range(3):
                total = total - base[block, d] * grads[(d + 1) * NODES : (d + 2) * NODES, lanes]
            for d in range(3):
                total = total - state[block, d] * base_grad[block, d, comp]
            acc[block, comp] = total

    def add_flux(block, fields, weights):
        for pair in range(SLOTS // 2):
            found = dot(fields, weights(pair))
            for k in (2 * pair, 2 * pair + 1):
                lanes = slice((k % 2) * LANES, (k % 2 + 1) * LANES)
                place = places[block, k]
                target = targets[block, k]
                lookups = jnp.bitwise_and(place, 7)
                origin = jnp.right_shift(place, 3)
                for comp in range(COMP):
                    at = 2 * comp * NODES
                    value = found[at : at + NODES, lanes]
                    value = value + found[at + NODES : at + 2 * NODES, lanes]
                    halves = []
                    for half, choices in enumerate(((0, 1, 2, 3, 6), (4, 5, 6, 7, 1))):
                        rows = slice(8 * half, 8 * half + 8)
                        picked = None
                        for choice in choices:
                            option = jnp.take_along_axis(
                                value[8 * choice : 8 * choice + 8], lookups[rows], axis=0
                            )
                            picked = (
                                option
                                if picked is None
                                else jnp.where(origin[rows] == choice, option, picked)
                            )
                        halves.append(picked)
                    for group in range(8):
                        rows = slice(8 * group, 8 * group + 8)
                        goal = target[rows]
                        spot = jnp.bitwise_and(goal, 7)
                        turned = jnp.where(
                            goal < 8,
                            jnp.take_along_axis(halves[0], spot, axis=0),
                            jnp.take_along_axis(halves[1], spot, axis=0),
                        )
                        acc[block, comp, rows] += jnp.where(goal < 16, turned, 0.0)

    def blend(low, high):
        return [jnp.where(lane_low, low(comp), high(comp)) for comp in range(COMP)]

    def block_field(block):
        return lambda comp: state[block, comp]

    def own_terms(block):
        pieces = pieces_of([state[block, comp] for comp in range(COMP)])
        sources[block, :, 0:LANES] = pieces
        local_terms(block, pieces)

    def own_flux(block):
        add_flux(block, sources[block], lambda pair: table[block, pair])

    def one_image(image):
        for block in range(2):
            own_terms(block)
        edge_sources[:, 0:LANES] = pieces_of(blend(block_field(0), block_field(1)))

        if image == 0:
            for index in range(3):
                for block in range(2):
                    list_copy(index, block).wait_recv()
            edge_lists()

        for side in range(2):
            across(
                state.at[side], halo.at[image], halo_send.at[image], halo_recv.at[image], 1 - side
            ).wait_recv()

        def halo_field(side):
            return lambda comp: halo[image, side, comp]

        sources[0, :, LANES:SHARD] = pieces_of(blend(block_field(1), halo_field(0)))
        sources[1, :, LANES:SHARD] = pieces_of(blend(halo_field(1), block_field(0)))
        for side in range(2):
            lanes = slice((side + 1) * LANES, (side + 2) * LANES)
            edge_sources[:, lanes] = pieces_of([halo[image, side, comp] for comp in range(COMP)])
        for block in range(2):
            own_flux(block)
        edge = blend(halo_field(1), halo_field(0))
        for comp in range(COMP):
            state[EDGE, comp] = edge[comp]

        if image == 0:
            for block in range(2):
                base_copy(block).wait_recv()
            kept = jnp.where(pack_low, base_far[1], base_far[0])
            other = pltpu.roll(jnp.where(pack_low, base_far[0], base_far[1]), HALO, 1)
            base[EDGE] = jnp.concatenate([kept, other], axis=0).reshape(COMP, NODES, LANES)
            base_gradient(EDGE)

        local_terms(EDGE, pieces_of(edge))
        add_flux(EDGE, edge_sources[...], lambda pair: edge_table[pair])
        for block in range(3):
            state[block] = state[block] + TIME_STEP * acc[block]

        for block in range(2):
            own_terms(block)
        sources[0, :, LANES:SHARD] = pieces_of(blend(block_field(1), block_field(EDGE)))
        sources[1, :, LANES:SHARD] = pieces_of(blend(block_field(EDGE), block_field(0)))
        for block in (1, 0):
            own_flux(block)
            arrival(image, block).wait_recv()
            lanes = block_lanes[block]
            value = state[block] + TIME_STEP * acc[block] - follow[image, :, :, lanes]
            (first_ref, second_ref)[image][:, :, lanes] = value
            if image == 0:
                state[block] = value
                halo_copy(1, block).start()
                follow_copy(1, block).start()

    for image in range(2):
        one_image(image)
    for block in range(2):
        for index in range(3):
            list_copy(index, block).wait_send()
        base_copy(block).wait_send()
        for image in range(2):
            halo_copy(image, block).wait_send()
    for image in range(2):
        for block in range(2):
            follow_copy(image, block).wait_send()


def on_device(base_flow, probe_field, neighbours, face_codes, face_counts):
    operators = operator_pieces()
    field = jax.ShapeDtypeStruct((COMP, NODES, SHARD), jnp.float32)
    vmem = pl.BlockSpec(memory_space=pltpu.VMEM)
    first_image, second_image = pl.pallas_call(
        functools.partial(kernel, lax.axis_size("seg"), lax.axis_size("elem")),
        out_shape=(field, field),
        in_specs=[pl.BlockSpec(memory_space=pltpu.HBM)] * 6,
        out_specs=(vmem, vmem),
        scratch_shapes=[
            pltpu.VMEM(operators.shape, jnp.bfloat16),
            pltpu.VMEM((SLOTS, SHARD), jnp.int32),
            pltpu.VMEM((SLOTS, SHARD), jnp.int32),
            pltpu.VMEM((1, SHARD), jnp.int32),
            pltpu.VMEM((2, SLOTS, LANES), jnp.int32),
            pltpu.VMEM((2, SLOTS, LANES), jnp.int32),
            pltpu.VMEM((2, 1, LANES), jnp.int32),
            pltpu.VMEM((3, COMP, NODES, LANES), jnp.float32),
            pltpu.VMEM((2, 96, LANES), jnp.float32),
            pltpu.VMEM((2, 96, LANES), jnp.float32),
            pltpu.VMEM((3, COMP, NODES, LANES), jnp.float32),
            pltpu.VMEM((3, COMP, NODES, LANES), jnp.float32),
            pltpu.VMEM((3, 3, COMP, NODES, LANES), jnp.float32),
            pltpu.VMEM((3, NODES, LANES), jnp.float32),
            pltpu.VMEM((3, SLOTS, 16, LANES), jnp.int32),
            pltpu.VMEM((3, SLOTS, NODES, LANES), jnp.int32),
            pltpu.VMEM((2, SLOTS // 2, SHARD, SHARD), jnp.bfloat16),
            pltpu.VMEM((SLOTS // 2, 3 * LANES, SHARD), jnp.bfloat16),
            pltpu.VMEM((2, 2 * COMP * NODES, SHARD), jnp.bfloat16),
            pltpu.VMEM((2 * COMP * NODES, 3 * LANES), jnp.bfloat16),
            pltpu.VMEM((2, 2, COMP, NODES, LANES), jnp.float32),
            pltpu.VMEM((2, COMP, NODES, SHARD), jnp.float32),
            pltpu.SemaphoreType.DMA((8,)),
            pltpu.SemaphoreType.DMA((3, 2)),
            pltpu.SemaphoreType.DMA((3, 2)),
            pltpu.SemaphoreType.DMA((2,)),
            pltpu.SemaphoreType.DMA((2,)),
            pltpu.SemaphoreType.DMA((2, 2)),
            pltpu.SemaphoreType.DMA((2, 2)),
            pltpu.SemaphoreType.DMA((2, 2)),
            pltpu.SemaphoreType.DMA((2, 2)),
        ],
        compiler_params=pltpu.CompilerParams(
            collective_id=0, has_side_effects=True, vmem_limit_bytes=40 * 1024 * 1024
        ),
        name="shooting",
    )(
        *[
            pltpu.with_memory_space_constraint(value, pltpu.HBM)
            for value in (
                base_flow[0],
                probe_field[0],
                neighbours,
                face_codes,
                face_counts.reshape(1, SHARD),
                operators,
            )
        ]
    )
    return (first_image[None], second_image[None])


def solution(mesh):
    placed = (
        P("seg", None, None, "elem"),
        P("seg", None, None, "elem"),
        P(None, "elem"),
        P(None, "elem"),
        P("elem"),
    )
    return jax.shard_map(
        on_device,
        mesh=mesh,
        in_specs=placed,
        out_specs=(P("seg", None, None, "elem"), P("seg", None, None, "elem")),
        check_vma=False,
    )
```

```python
import functools

import jax
import jax.numpy as jnp
import ml_dtypes
import numpy as np
from jax import lax
from jax.experimental import pallas as pl
from jax.experimental.pallas import tpu as pltpu
from jax.sharding import PartitionSpec as P

STEPS = 2
VISCOSITY = 0.05
PENALTY = 1.0
TIME_STEP = 0.05

COMP = 3
NODES = 64
SHARD = 256
LANES = 128
HALO = 64
EDGE = 2
SLOTS = 6


def operator_tables():
    points = np.array([-1.0, -1.0 / np.sqrt(5.0), 1.0 / np.sqrt(5.0), 1.0])
    barycentric = np.array(
        [
            1.0 / np.prod([points[row] - points[col] for col in range(4) if col != row])
            for row in range(4)
        ]
    )
    derivative = np.zeros((4, 4))
    for row in range(4):
        for col in range(4):
            if row != col:
                derivative[row, col] = (
                    barycentric[col] / barycentric[row] / (points[row] - points[col])
                )
        derivative[row, row] = -np.sum(derivative[row])
    identity = np.eye(4)
    gradient = [
        np.kron(np.kron(derivative, identity), identity),
        np.kron(np.kron(identity, derivative), identity),
        np.kron(np.kron(identity, identity), derivative),
    ]
    laplacian = sum(table @ table for table in gradient)
    return gradient, laplacian


def operator_pieces():
    gradient, laplacian = operator_tables()
    stacked = np.concatenate([VISCOSITY * laplacian] + gradient, axis=0)
    high = stacked.astype(ml_dtypes.bfloat16)
    low = (stacked - high.astype(np.float64)).astype(ml_dtypes.bfloat16)
    return jnp.asarray(np.concatenate([high, high, low, low], axis=1))


def split(value):
    high = value.astype(jnp.bfloat16)
    low = (value - high.astype(jnp.float32)).astype(jnp.bfloat16)
    return high, low


def dot(left, right):
    return jnp.dot(left, right, preferred_element_type=jnp.float32)


def kernel(
    segs,
    elems,
    base_in,
    probe_in,
    near_in,
    code_in,
    count_in,
    oper_in,
    first_ref,
    second_ref,
    oper_ref,
    near_ref,
    code_ref,
    count_ref,
    near_far,
    code_far,
    count_far,
    base,
    base_pack,
    base_far,
    state,
    acc,
    base_grad,
    own_count,
    places,
    targets,
    table,
    edge_table,
    sources,
    edge_sources,
    halo,
    follow,
    input_sem,
    list_send,
    list_recv,
    base_send,
    base_recv,
    halo_send,
    halo_recv,
    follow_send,
    follow_recv,
):
    seg = lax.axis_index("seg")
    elem = lax.axis_index("elem")
    right = lax.rem(elem + 1, elems)
    left = lax.rem(elem + elems - 1, elems)
    ahead = lax.rem(seg + 1, segs)
    behind = lax.rem(seg + segs - 1, segs)
    barrier = pltpu.get_barrier_semaphore()
    for target in ({"elem": left}, {"elem": right}, {"seg": ahead}):
        pl.semaphore_signal(
            barrier, inc=1, device_id=target, device_id_type=pl.DeviceIdType.MESH
        )
    block_lanes = (slice(0, LANES), slice(LANES, SHARD))
    pairs = [(near_in, near_ref), (code_in, code_ref), (count_in, count_ref)]
    for block in range(2):
        pairs.append((probe_in.at[:, :, block_lanes[block]], state.at[block]))
    for block in range(2):
        pairs.append((base_in.at[:, :, block_lanes[block]], base.at[block]))
    pairs.append((oper_in, oper_ref))
    loads = [
        pltpu.make_async_copy(source, target, input_sem.at[index])
        for index, (source, target) in enumerate(pairs)
    ]
    for load in loads:
        load.start()

    def across(source, target, send, recv, block):
        return pltpu.make_async_remote_copy(
            src_ref=source,
            dst_ref=target.at[1 - block],
            send_sem=send.at[block],
            recv_sem=recv.at[1 - block],
            device_id={"elem": (left, right)[block]},
            device_id_type=pl.DeviceIdType.MESH,
        )

    def list_copy(index, block):
        source, target = (
            (near_in, near_far),
            (code_in, code_far),
            (count_in, count_far),
        )[index]
        source = source.at[:, block_lanes[block]]
        return across(source, target, list_send.at[index], list_recv.at[index], block)

    def base_copy(block):
        return across(base_pack.at[block], base_far, base_send, base_recv, block)

    def halo_copy(image, block):
        source = (probe_in, first_ref)[image].at[:, :, block_lanes[block]]
        return across(source, halo.at[image], halo_send.at[image], halo_recv.at[image], block)

    def follow_copy(image, block):
        return arrival(image, block, (probe_in, first_ref)[image])

    def arrival(image, block, source=first_ref):
        lanes = block_lanes[block]
        return pltpu.make_async_remote_copy(
            src_ref=source.at[:, :, lanes],
            dst_ref=follow.at[image, :, :, lanes],
            send_sem=follow_send.at[image, block],
            recv_sem=follow_recv.at[image, block],
            device_id={"seg": behind},
            device_id_type=pl.DeviceIdType.MESH,
        )

    pl.semaphore_wait(barrier, 3)
    for index in range(3):
        for block in range(2):
            list_copy(index, block).start()
    for block in range(2):
        halo_copy(0, block).start()

    lane_low = lax.broadcasted_iota(jnp.int32, (NODES, LANES), 1) < HALO
    pack_low = lax.broadcasted_iota(jnp.int32, (96, LANES), 1) < HALO
    list_low = lax.broadcasted_iota(jnp.int32, (SLOTS, LANES), 1) < HALO
    row = lax.broadcasted_iota(jnp.int32, (LANES, LANES), 0)
    slot = lax.broadcasted_iota(jnp.int32, (SLOTS, LANES), 0)
    node = lax.broadcasted_iota(jnp.int32, (NODES, LANES), 0)
    node_at = (
        jnp.right_shift(node, 4),
        jnp.bitwise_and(jnp.right_shift(node, 2), 3),
        jnp.bitwise_and(node, 3),
    )
    trace = lax.broadcasted_iota(jnp.int32, (16, LANES), 0)
    trace_i, trace_j = jnp.right_shift(trace, 2), jnp.bitwise_and(trace, 3)
    blocks = elems * (SHARD // LANES)
    first_block = elem * (SHARD // LANES)

    def one_hot(chosen):
        return jnp.where(row == chosen, 1.0, 0.0).astype(jnp.bfloat16)

    def index_nodes(block, code, live):
        total = jnp.zeros((NODES, LANES), jnp.float32)
        for k in range(SLOTS):
            at = code[k : k + 1]
            way = jnp.right_shift(at, 3)
            end = 3 * jnp.bitwise_and(jnp.right_shift(at, 2), 1)
            turn = jnp.bitwise_and(at, 3)
            far = 3 - end
            place = jnp.where(
                way == 0,
                16 * far + 4 * trace_i + trace_j,
                jnp.where(
                    way == 1,
                    16 * trace_i + 4 * far + trace_j,
                    16 * trace_i + 4 * trace_j + far,
                ),
            )
            places[block, k] = place
            along = jnp.where(way == 0, node_at[0], jnp.where(way == 1, node_at[1], node_at[2]))
            i = jnp.where(way == 0, node_at[1], node_at[0])
            j = jnp.where(way == 2, node_at[1], node_at[2])
            odd = jnp.bitwise_and(turn, 1) == 1
            turned_i, turned_j = jnp.where(odd, j, i), jnp.where(odd, i, j)
            turned_i = jnp.where(turn >= 2, 3 - turned_i, turned_i)
            flip = jnp.logical_or(turn == 1, turn == 2)
            turned_j = jnp.where(flip, 3 - turned_j, turned_j)
            wanted = jnp.where(live[k : k + 1] == 1, end, -1)
            member = along == wanted
            targets[block, k] = jnp.where(member, 4 * turned_i + turned_j, 16)
            total = total + jnp.where(member, 1.0, 0.0)
        own_count[block] = total

    for load in loads[0:3]:
        load.wait()

    def own_lists(block):
        lanes = block_lanes[block]
        near = near_ref[:, lanes]
        used = slot < count_ref[:, lanes]
        place = jnp.where(used, jnp.bitwise_and(near, LANES - 1), -1)
        is_own = jnp.right_shift(near, 7) == first_block + block
        inside, beyond = jnp.where(is_own, place, -1), jnp.where(is_own, -1, place)
        for k in range(SLOTS):
            columns = slice((k % 2) * LANES, (k % 2 + 1) * LANES)
            table[block, k // 2, 0:LANES, columns] = one_hot(inside[k : k + 1])
            table[block, k // 2, LANES:SHARD, columns] = one_hot(beyond[k : k + 1])
        index_nodes(block, code_ref[:, lanes], jnp.where(used, 1, 0))

    def edge_lists():
        near = jnp.where(list_low, near_far[1], near_far[0])
        code = jnp.where(list_low, code_far[1], code_far[0])
        used = slot < jnp.where(list_low[0:1], count_far[1], count_far[0])
        place = jnp.where(used, jnp.bitwise_and(near, LANES - 1), -1)
        outer = jnp.where(
            list_low, lax.rem(first_block + 2, blocks), lax.rem(first_block + blocks - 1, blocks)
        )
        is_outer = jnp.right_shift(near, 7) == outer
        inside, beyond = jnp.where(is_outer, -1, place), jnp.where(is_outer, place, -1)
        to_left, to_right = jnp.where(list_low, -1, beyond), jnp.where(list_low, beyond, -1)
        for k in range(SLOTS):
            columns = slice((k % 2) * LANES, (k % 2 + 1) * LANES)
            for part, chosen in enumerate((inside, to_left, to_right)):
                rows = slice(part * LANES, (part + 1) * LANES)
                edge_table[k // 2, rows, columns] = one_hot(chosen[k : k + 1])
        index_nodes(EDGE, code, jnp.where(used, 1, 0))

    for load in loads[5:7]:
        load.wait()
    for block in range(2):
        packed = base[block].reshape(COMP * NODES, LANES)
        upper, lower = packed[0:96], pltpu.roll(packed[96:192], HALO, 1)
        base_pack[block] = (
            jnp.where(pack_low, upper, lower) if block == 0 else jnp.where(pack_low, lower, upper)
        )
        base_copy(block).start()
    for block in (1, 0):
        follow_copy(0, block).start()
    for block in range(2):
        own_lists(block)

    def pieces_of(fields):
        return jnp.concatenate([piece for field in fields for piece in split(field)], axis=0)

    def derivatives(pieces):
        width = 2 * NODES
        beside = jnp.concatenate(
            [pieces[comp * width : (comp + 1) * width] for comp in range(COMP)], axis=1
        )
        return dot(oper_ref[...], jnp.concatenate([beside, beside], axis=0))

    def base_gradient(block):
        grads = derivatives(pieces_of([base[block, comp] for comp in range(COMP)]))
        for comp in range(COMP):
            lanes = slice(comp * LANES, (comp + 1) * LANES)
            for d in range(3):
                base_grad[block, d, comp] = grads[(d + 1) * NODES : (d + 2) * NODES, lanes]

    loads[7].wait()
    for block in range(2):
        base_gradient(block)
    for load in loads[3:5]:
        load.wait()

    def local_terms(block, pieces):
        grads = derivatives(pieces)
        for comp in range(COMP):
            lanes = slice(comp * LANES, (comp + 1) * LANES)
            total = grads[0:NODES, lanes] - own_count[block] * state[block, comp]
            for d in range(3):
                total = total - base[block, d] * grads[(d + 1) * NODES : (d + 2) * NODES, lanes]
            for d in range(3):
                total = total - state[block, d] * base_grad[block, d, comp]
            acc[block, comp] = total

    def add_flux(block, fields, weights):
        for pair in range(SLOTS // 2):
            found = dot(fields, weights(pair))
            for k in (2 * pair, 2 * pair + 1):
                lanes = slice((k % 2) * LANES, (k % 2 + 1) * LANES)
                place = places[block, k]
                target = targets[block, k]
                lookups = jnp.bitwise_and(place, 7)
                origin = jnp.right_shift(place, 3)
                for comp in range(COMP):
                    at = 2 * comp * NODES
                    value = found[at : at + NODES, lanes]
                    value = value + found[at + NODES : at + 2 * NODES, lanes]
                    halves = []
                    for half, choices in enumerate(((0, 1, 2, 3, 6), (4, 5, 6, 7, 1))):
                        rows = slice(8 * half, 8 * half + 8)
                        picked = None
                        for choice in choices:
                            option = jnp.take_along_axis(
                                value[8 * choice : 8 * choice + 8], lookups[rows], axis=0
                            )
                            picked = (
                                option
                                if picked is None
                                else jnp.where(origin[rows] == choice, option, picked)
                            )
                        halves.append(picked)
                    for group in range(8):
                        rows = slice(8 * group, 8 * group + 8)
                        goal = target[rows]
                        spot = jnp.bitwise_and(goal, 7)
                        turned = jnp.where(
                            goal < 8,
                            jnp.take_along_axis(halves[0], spot, axis=0),
                            jnp.take_along_axis(halves[1], spot, axis=0),
                        )
                        acc[block, comp, rows] += jnp.where(goal < 16, turned, 0.0)

    def blend(low, high):
        return [jnp.where(lane_low, low(comp), high(comp)) for comp in range(COMP)]

    def block_field(block):
        return lambda comp: state[block, comp]

    def own_terms(block):
        pieces = pieces_of([state[block, comp] for comp in range(COMP)])
        sources[block, :, 0:LANES] = pieces
        local_terms(block, pieces)

    def own_flux(block):
        add_flux(block, sources[block], lambda pair: table[block, pair])

    def one_image(image):
        for block in range(2):
            own_terms(block)
        edge_sources[:, 0:LANES] = pieces_of(blend(block_field(0), block_field(1)))

        if image == 0:
            for index in range(3):
                for block in range(2):
                    list_copy(index, block).wait_recv()
            edge_lists()

        def halo_field(side):
            return lambda comp: halo[image, side, comp]

        for side in (1, 0):
            across(
                state.at[side], halo.at[image], halo_send.at[image], halo_recv.at[image], 1 - side
            ).wait_recv()
            low, high = block_field(1), halo_field(0)
            if side == 1:
                low, high = halo_field(1), block_field(0)
            sources[side, :, LANES:SHARD] = pieces_of(blend(low, high))
            lanes = slice((side + 1) * LANES, (side + 2) * LANES)
            edge_sources[:, lanes] = pieces_of([halo[image, side, comp] for comp in range(COMP)])
            own_flux(side)
        edge = blend(halo_field(1), halo_field(0))
        for comp in range(COMP):
            state[EDGE, comp] = edge[comp]

        if image == 0:
            for block in range(2):
                base_copy(block).wait_recv()
            kept = jnp.where(pack_low, base_far[1], base_far[0])
            other = pltpu.roll(jnp.where(pack_low, base_far[0], base_far[1]), HALO, 1)
            base[EDGE] = jnp.concatenate([kept, other], axis=0).reshape(COMP, NODES, LANES)
            base_gradient(EDGE)

        local_terms(EDGE, pieces_of(edge))
        add_flux(EDGE, edge_sources[...], lambda pair: edge_table[pair])
        for block in range(3):
            state[block] = state[block] + TIME_STEP * acc[block]

        for block in range(2):
            own_terms(block)
        sources[0, :, LANES:SHARD] = pieces_of(blend(block_field(1), block_field(EDGE)))
        sources[1, :, LANES:SHARD] = pieces_of(blend(block_field(EDGE), block_field(0)))
        for block in (1, 0):
            own_flux(block)
            arrival(image, block).wait_recv()
            lanes = block_lanes[block]
            value = state[block] + TIME_STEP * acc[block] - follow[image, :, :, lanes]
            (first_ref, second_ref)[image][:, :, lanes] = value
            if image == 0:
                state[block] = value
                halo_copy(1, block).start()
                follow_copy(1, block).start()

    for image in range(2):
        one_image(image)
    for block in range(2):
        for index in range(3):
            list_copy(index, block).wait_send()
        base_copy(block).wait_send()
        for image in range(2):
            halo_copy(image, block).wait_send()
    for image in range(2):
        for block in range(2):
            follow_copy(image, block).wait_send()


def on_device(base_flow, probe_field, neighbours, face_codes, face_counts):
    operators = operator_pieces()
    field = jax.ShapeDtypeStruct((COMP, NODES, SHARD), jnp.float32)
    vmem = pl.BlockSpec(memory_space=pltpu.VMEM)
    first_image, second_image = pl.pallas_call(
        functools.partial(kernel, lax.axis_size("seg"), lax.axis_size("elem")),
        out_shape=(field, field),
        in_specs=[pl.BlockSpec(memory_space=pltpu.HBM)] * 6,
        out_specs=(vmem, vmem),
        scratch_shapes=[
            pltpu.VMEM(operators.shape, jnp.bfloat16),
            pltpu.VMEM((SLOTS, SHARD), jnp.int32),
            pltpu.VMEM((SLOTS, SHARD), jnp.int32),
            pltpu.VMEM((1, SHARD), jnp.int32),
            pltpu.VMEM((2, SLOTS, LANES), jnp.int32),
            pltpu.VMEM((2, SLOTS, LANES), jnp.int32),
            pltpu.VMEM((2, 1, LANES), jnp.int32),
            pltpu.VMEM((3, COMP, NODES, LANES), jnp.float32),
            pltpu.VMEM((2, 96, LANES), jnp.float32),
            pltpu.VMEM((2, 96, LANES), jnp.float32),
            pltpu.VMEM((3, COMP, NODES, LANES), jnp.float32),
            pltpu.VMEM((3, COMP, NODES, LANES), jnp.float32),
            pltpu.VMEM((3, 3, COMP, NODES, LANES), jnp.float32),
            pltpu.VMEM((3, NODES, LANES), jnp.float32),
            pltpu.VMEM((3, SLOTS, 16, LANES), jnp.int32),
            pltpu.VMEM((3, SLOTS, NODES, LANES), jnp.int32),
            pltpu.VMEM((2, SLOTS // 2, SHARD, SHARD), jnp.bfloat16),
            pltpu.VMEM((SLOTS // 2, 3 * LANES, SHARD), jnp.bfloat16),
            pltpu.VMEM((2, 2 * COMP * NODES, SHARD), jnp.bfloat16),
            pltpu.VMEM((2 * COMP * NODES, 3 * LANES), jnp.bfloat16),
            pltpu.VMEM((2, 2, COMP, NODES, LANES), jnp.float32),
            pltpu.VMEM((2, COMP, NODES, SHARD), jnp.float32),
            pltpu.SemaphoreType.DMA((8,)),
            pltpu.SemaphoreType.DMA((3, 2)),
            pltpu.SemaphoreType.DMA((3, 2)),
            pltpu.SemaphoreType.DMA((2,)),
            pltpu.SemaphoreType.DMA((2,)),
            pltpu.SemaphoreType.DMA((2, 2)),
            pltpu.SemaphoreType.DMA((2, 2)),
            pltpu.SemaphoreType.DMA((2, 2)),
            pltpu.SemaphoreType.DMA((2, 2)),
        ],
        compiler_params=pltpu.CompilerParams(
            collective_id=0, has_side_effects=True, vmem_limit_bytes=40 * 1024 * 1024
        ),
        name="shooting",
    )(
        *[
            pltpu.with_memory_space_constraint(value, pltpu.HBM)
            for value in (
                base_flow[0],
                probe_field[0],
                neighbours,
                face_codes,
                face_counts.reshape(1, SHARD),
                operators,
            )
        ]
    )
    return (first_image[None], second_image[None])


def solution(mesh):
    placed = (
        P("seg", None, None, "elem"),
        P("seg", None, None, "elem"),
        P(None, "elem"),
        P(None, "elem"),
        P("elem"),
    )
    return jax.shard_map(
        on_device,
        mesh=mesh,
        in_specs=placed,
        out_specs=(P("seg", None, None, "elem"), P("seg", None, None, "elem")),
        check_vma=False,
    )
```
